128 devices in a mesh: blk: 32 (over z, y, core), sub: 4 (over x).
Axes of the slice: x: 4, y: 4, z: 4, core: 2. Of those that a mesh axis runs over, the one named last changes fastest.
Arguments:
- dynamics_profile_values: float32 [131072, 768], P(('blk', 'sub')), may hold values from -6 to 6
- parameterized_increments: float32 [131072, 768], P(('blk', 'sub')), may hold values from -4 to 4
- ground_exchange_rates: float32 [6, 131072], P(None, ('blk', 'sub')), may hold values from -6 to 6
- sunlit_indicator: int32 [131072], P(('blk', 'sub')), may hold values 0 or 1
- eddy_coefficient_scale: float32 [131072], P(('blk', 'sub')), may hold values from 0.05 to 100
- departing_profile_indices: int32 [128, 128, 8], P(('blk', 'sub')), may hold values from 0 to 1024, as said below
- arriving_parcel_places: int32 [128, 128, 8], P(('blk', 'sub')), may hold values from 0 to 1024, as said below
- resident_parcel_place: int32 [128, 1024], P(('blk', 'sub')), may hold values from 0 to 1024, as said below
- boundary_profile_indices: int32 [128, 2, 128], P(('blk', 'sub')), may hold values from 0 to 1023, as said below
Outputs:
- span_state: float32 [131072, 768], P(('blk', 'sub'))
- column_result: float32 [131072, 768], P(('blk', 'sub'))
The draws below stay inside these ranges and needn't reach their ends.
Inputs may be any that keep to these rules, and one draw needn't show every extreme that they name: departing_profile_indices[n, p] names distinct own columns of device n that go to device p, then 1024 in the empty slots; no column is named twice for n and none stays named for p = n. The number of columns n sends to (n + o) mod 128 is between 1 and 8 for o ≠ 0, depends only on o, is 8 for some o and 1 for another. arriving_parcel_places[p, n, c] is the span position on device p of the column in departing_profile_indices[n, p, c], or 1024 exactly where that slot is empty. resident_parcel_place[n, j] is the span position on device n of its own column j if that column stays, else 1024 (exactly for the columns named in departing_profile_indices[n]); with arriving_parcel_places, every span position of every device is filled exactly once. boundary_profile_indices[n] names 256 distinct columns of device n; left point k of device b * 4 + s is the same grid point as right point k of device ((b - 1) mod 32) * 4 + s.
All inputs are finite; a program needn't handle non-finite values. No bound on the sum of `sunlit_indicator` on one device may be relied on, other than what follows from the above.
Results may differ from the reference program's by a relative error of at most 0.000066.
Values sent between devices are 32-bit elements; how exact they have to be, the bound alone decides.
No kernel may reach another device: no remote copies, remote signals or barrier semaphores. Data moves between devices by JAX's collectives and lax.ppermute only.
A program may use at most 128 MiB of HBM per device.

```python
import math
import jax
import jax.numpy as jnp
from jax import lax

MIXED_QUANTITIES = 6
LEV = 128
PROFILES_ON_UNIT = 1024
CAP = 8
EDGE = 128
GLOBAL_PROFILES = 131072
N_BLK = 32
N_SUB = 4
DEVICES = 128


def column_maps(key):
    folded = jax.random.fold_in(key, 101)
    k_count, k_pick, k_source, k_target = jax.random.split(folded, 4)
    everyone = jnp.arange(DEVICES, dtype=jnp.int32)
    counts = jax.random.randint(k_count, (DEVICES,), 1, CAP + 1, dtype=jnp.int32)
    picked = jax.random.permutation(k_pick, DEVICES - 1) + 1
    counts = counts.at[picked[0]].set(CAP).at[picked[1]].set(1).at[0].set(0)
    starts = jnp.cumsum(counts) - counts
    moved_total = jnp.sum(counts)
    source_order = jax.vmap(lambda one_key: jax.random.permutation(one_key, PROFILES_ON_UNIT))(jax.random.split(k_source, DEVICES)).astype(jnp.int32)
    target_order = jax.vmap(lambda one_key: jax.random.permutation(one_key, PROFILES_ON_UNIT))(jax.random.split(k_target, DEVICES)).astype(jnp.int32)
    offset = (everyone[None, :] - everyone[:, None]) % DEVICES
    slot_ids = jnp.arange(CAP, dtype=jnp.int32)
    occupied = slot_ids[None, None, :] < counts[offset][:, :, None]
    position = jnp.minimum(starts[offset][:, :, None] + slot_ids[None, None, :], PROFILES_ON_UNIT - 1)
    sending = jnp.where(occupied, source_order[everyone[:, None, None], position], PROFILES_ON_UNIT)
    landed = jnp.where(occupied, target_order[everyone[None, :, None], position], PROFILES_ON_UNIT)
    ranking = jnp.argsort(source_order, axis=1).astype(jnp.int32)
    staying = jnp.where(ranking >= moved_total, jnp.take_along_axis(target_order, ranking, axis=1), PROFILES_ON_UNIT)
    return (sending.astype(jnp.int32), jnp.transpose(landed, (1, 0, 2)).astype(jnp.int32), staying.astype(jnp.int32))


def draw_departing_profile_indices(key, part):
    return column_maps(key)[0]


def draw_arriving_parcel_places(key, part):
    return column_maps(key)[1]


def draw_resident_parcel_place(key, part):
    return column_maps(key)[2]


def draw_boundary_profile_indices(key, part):
    folded = jax.random.fold_in(key, 202)
    orders = jax.vmap(lambda one_key: jax.random.permutation(one_key, PROFILES_ON_UNIT))(jax.random.split(folded, DEVICES)).astype(jnp.int32)
    return orders[:, :2 * EDGE].reshape(DEVICES, 2, EDGE)


def plant(values, own_key, least, top_value):
    longest = values.shape.index(max(values.shape))
    spots = []
    for shift in (0, 1):
        where = [jax.random.randint(jax.random.fold_in(own_key, axis), (), 0, length) for axis, length in enumerate(values.shape)]
        where[longest] = (where[longest] + shift) % values.shape[longest]
        spots.append(tuple(where))
    return values.at[spots[0]].set(least).at[spots[1]].set(top_value)


def steps_of(stream_key, extent, shards, least, high):
    gain, own = 1.0, jax.random.fold_in(stream_key, 6)
    for dim, shards_of in shards:
        draws = jnp.exp(jax.random.uniform(jax.random.fold_in(own, dim), (shards_of,), jnp.float32, least / len(shards), high / len(shards)))
        gain = gain * jnp.repeat(draws, extent[dim] // shards_of).reshape([-1 if axis == dim else 1 for axis in range(len(extent))])
    return gain


def gaussian(key, extent, width, reach, cuts=(), kind=jnp.bfloat16):
    factor_of = steps_of(key, extent, cuts, -0.22, 0.18) if cuts else 1.0
    values = jax.random.normal(key, extent, jnp.float32) * width * factor_of
    return jnp.minimum(jnp.maximum(values, -reach), reach).astype(kind)


def setup_inputs(seed: int = 0) -> dict:
    key_list = jax.random.split(jax.random.key(seed), 10)
    return {
        "dynamics_profile_values": gaussian(key_list[0], (GLOBAL_PROFILES, MIXED_QUANTITIES * LEV), 1.0, 6.0, ((0, 128),), jnp.float32),
        "parameterized_increments": gaussian(key_list[1], (GLOBAL_PROFILES, MIXED_QUANTITIES * LEV), 0.5, 4.0, ((0, 128),), jnp.float32),
        "ground_exchange_rates": gaussian(key_list[2], (MIXED_QUANTITIES, GLOBAL_PROFILES), 1.0, 6.0, ((1, 128),), jnp.float32),
        "sunlit_indicator": plant((jax.random.randint(key_list[3], (GLOBAL_PROFILES,), 0, 2) < 1).astype(jnp.int32), jax.random.fold_in(key_list[3], 1), 0, 1),
        "eddy_coefficient_scale": jnp.clip(jnp.exp(math.log(100.0) - 7.6009024 * jax.random.uniform(key_list[4], (GLOBAL_PROFILES,), jnp.float32) ** steps_of(key_list[4], (GLOBAL_PROFILES,), ((0, 128),), -0.2, 0.2)), 0.05, 100.0),
        "departing_profile_indices": draw_departing_profile_indices(jax.random.fold_in(key_list[9], 71), 0),
        "arriving_parcel_places": draw_arriving_parcel_places(jax.random.fold_in(key_list[9], 71), 0),
        "resident_parcel_place": draw_resident_parcel_place(jax.random.fold_in(key_list[9], 71), 0),
        "boundary_profile_indices": draw_boundary_profile_indices(jax.random.fold_in(key_list[9], 71), 0),
    }


def from_below(values, stride, padding):
    border = jnp.full(values.shape[:-1] + (stride,), padding, values.dtype)
    return jnp.concatenate([border, values[..., :-stride]], axis=-1)


def from_above(values, stride, padding):
    border = jnp.full(values.shape[:-1] + (stride,), padding, values.dtype)
    return jnp.concatenate([values[..., stride:], border], axis=-1)


def tridiagonal(weights, right_side):
    border = jnp.zeros(weights.shape[:-1] + (1,), jnp.float32)
    weight_below = jnp.concatenate([border, weights], axis=-1)[:, None, :]
    weight_above = jnp.concatenate([weights, border], axis=-1)[:, None, :]
    below_coef = -weight_below
    above_coef = -weight_above
    diagonal = 1.0 + weight_below + weight_above
    levels = weights.shape[-1] + 1
    stride = 1
    while stride < levels:
        lower_factor = -below_coef / from_below(diagonal, stride, 1.0)
        upper_factor = -above_coef / from_above(diagonal, stride, 1.0)
        new_diagonal = diagonal + lower_factor * from_below(above_coef, stride, 0.0) + upper_factor * from_above(below_coef, stride, 0.0)
        right_side = right_side + lower_factor * from_below(right_side, stride, 0.0) + upper_factor * from_above(right_side, stride, 0.0)
        below_coef = lower_factor * from_below(below_coef, stride, 0.0)
        above_coef = upper_factor * from_above(above_coef, stride, 0.0)
        diagonal = new_diagonal
        stride = stride * 2
    return right_side / diagonal


def parameterization_update(profile_levels_count, parameterized_increments, profile_forcing_increment, eddy_coefficient_scale):
    count_rows = profile_levels_count.shape[0]
    fields = profile_levels_count.reshape(count_rows, MIXED_QUANTITIES, LEV)
    potential = fields[:, 0]
    zonal = fields[:, 2]
    meridional = fields[:, 3]
    lapse = potential[:, :-1] - potential[:, 1:]
    shear_sq = (zonal[:, :-1] - zonal[:, 1:]) ** 2 + (meridional[:, :-1] - meridional[:, 1:]) ** 2 + 0.1
    richardson = lapse / shear_sq
    stable_part = jnp.maximum(richardson, 0.0)
    unstable_part = jnp.minimum(richardson, 0.0)
    buoyancy_frequency_squared = (1.0 - 8.0 * unstable_part) / ((1.0 - unstable_part) * (1.0 + 10.0 * stable_part) ** 2)
    viscosity_coefficient = eddy_coefficient_scale[:, None] * buoyancy_frequency_squared
    heat_k = 1.35 * viscosity_coefficient
    right_side = fields + parameterized_increments.reshape(count_rows, MIXED_QUANTITIES, LEV)
    right_side = right_side.at[:, :, LEV - 1].add(profile_forcing_increment)
    heat_fields = tridiagonal(heat_k, jnp.concatenate([right_side[:, 0:2], right_side[:, 4:6]], axis=1))
    wind_fields = tridiagonal(viscosity_coefficient, right_side[:, 2:4])
    result = jnp.concatenate([heat_fields[:, 0:2], wind_fields, heat_fields[:, 2:4]], axis=1)
    return result.reshape(count_rows, MIXED_QUANTITIES * LEV)


def reference(dynamics_profile_values, parameterized_increments, ground_exchange_rates, sunlit_indicator, eddy_coefficient_scale, departing_profile_indices, arriving_parcel_places, resident_parcel_place, boundary_profile_indices):
    everyone = jnp.arange(DEVICES, dtype=jnp.int32)
    parcel_breadth = MIXED_QUANTITIES * LEV
    anchor_sent = jnp.where(departing_profile_indices < PROFILES_ON_UNIT, everyone[:, None, None] * PROFILES_ON_UNIT + departing_profile_indices, GLOBAL_PROFILES)
    landing = jnp.transpose(arriving_parcel_places, (1, 0, 2))
    target_sent = jnp.where(landing < PROFILES_ON_UNIT, everyone[None, :, None] * PROFILES_ON_UNIT + landing, GLOBAL_PROFILES)
    anchor_kept = everyone[:, None] * PROFILES_ON_UNIT + jnp.arange(PROFILES_ON_UNIT, dtype=jnp.int32)[None, :]
    target_kept = jnp.where(resident_parcel_place < PROFILES_ON_UNIT, everyone[:, None] * PROFILES_ON_UNIT + resident_parcel_place, GLOBAL_PROFILES)
    targets = jnp.concatenate([target_kept.reshape(-1), target_sent.reshape(-1)]).astype(jnp.int32)
    sources = jnp.concatenate([anchor_kept.reshape(-1), anchor_sent.reshape(-1)]).astype(jnp.int32)
    anchor = jnp.zeros((GLOBAL_PROFILES + 1,), jnp.int32).at[targets].set(sources)[:GLOBAL_PROFILES]
    parcel_gather = dynamics_profile_values[anchor]
    profile_forcing_increment = ground_exchange_rates * (0.5 + sunlit_indicator.astype(jnp.float32))
    partition_segments = (parcel_gather.reshape(DEVICES, PROFILES_ON_UNIT, parcel_breadth), parameterized_increments.reshape(DEVICES, PROFILES_ON_UNIT, parcel_breadth), jnp.transpose(profile_forcing_increment).reshape(DEVICES, PROFILES_ON_UNIT, MIXED_QUANTITIES), eddy_coefficient_scale.reshape(DEVICES, PROFILES_ON_UNIT))
    parcel_scatter = lax.map(lambda group: parameterization_update(group[0], group[1], group[2], group[3]), partition_segments).reshape(GLOBAL_PROFILES, parcel_breadth)
    column_out = jnp.zeros((GLOBAL_PROFILES, parcel_breadth), jnp.float32).at[anchor].set(parcel_scatter)
    previous = ((everyone // N_SUB - 1) % N_BLK) * N_SUB + everyone % N_SUB
    left_points = (everyone[:, None] * PROFILES_ON_UNIT + boundary_profile_indices[:, 0, :]).reshape(-1)
    right_points = (everyone[:, None] * PROFILES_ON_UNIT + boundary_profile_indices[:, 1, :])[previous].reshape(-1)
    averaged = (column_out[left_points] + column_out[right_points]) * 0.5
    column_out = column_out.at[left_points].set(averaged).at[right_points].set(averaged)
    return parcel_scatter, column_out
```

```python
import functools

import jax
import jax.numpy as jnp
from jax import lax
from jax.experimental import pallas as pl
from jax.experimental.pallas import tpu as pltpu
from jax.sharding import PartitionSpec as P

FIELDS = 6
LEV = 128
COLS = 1024
PEERS = 128
CAP = 8
EDGE = 128
ROW = 7
DUMP = COLS
ROWS_ALLOC = 7176
X_PART = CAP * FIELDS
MESSAGE = X_PART + CAP * ROW
GROUP = 137
VMEM_LIMIT = 60 * 2**20
HEAT = (0, 1, 4, 5)
RICHARDSON = {0: 0, 2: 1, 3: 2}


def to_tiles(rows):
    return rows.reshape(COLS // 8, 8, FIELDS, LEV).transpose(0, 2, 1, 3).reshape(COLS * FIELDS, LEV)


def from_tiles(tiles):
    return tiles.reshape(COLS // 8, FIELDS, 8, LEV).transpose(0, 2, 1, 3).reshape(COLS, FIELDS * LEV)


def spread_rows(tiles, rows):
    def body(t, carry):
        for f in range(FIELDS):
            rows[pl.ds(t * 8 * ROW + f, 8, stride=ROW), :] = tiles[pl.ds(t * 48 + f * 8, 8), :]
        return carry

    lax.fori_loop(0, COLS // 8, body, 0, unroll=4)


def spread_scalars(scalars, rows):
    for g in range(8):
        part = scalars[:, g * 128 : (g + 1) * 128]
        square = jnp.concatenate([part] * 16, axis=0).T
        for i in range(16):
            rows[pl.ds((g * 128 + i * 8) * ROW + FIELDS, 8, stride=ROW), :] = square[i * 8 : (i + 1) * 8]


def pack_kernel(departing, arriving, x, inc, scalars, send, x_rows, inc_rows):
    spread_rows(x, x_rows)
    spread_rows(inc, inc_rows)
    spread_scalars(scalars, inc_rows)

    def body(p, carry):
        for c in range(CAP):
            j = jnp.minimum(departing[p * CAP + c], COLS - 1)
            send[pl.ds(p * MESSAGE + c * FIELDS, FIELDS), :] = x_rows[pl.ds(j * ROW, FIELDS), :]
        for c in range(CAP):
            q = jnp.minimum(arriving[p * CAP + c], COLS - 1)
            send[pl.ds(p * MESSAGE + X_PART + c * ROW, ROW), :] = inc_rows[pl.ds(q * ROW, ROW), :]
        return carry

    lax.fori_loop(0, PEERS, body, 0)


def resident_kernel(staying, x, inc, scalars, span_x, block_inc, x_rows, inc_rows):
    spread_rows(x, x_rows)
    spread_rows(inc, inc_rows)
    spread_scalars(scalars, inc_rows)

    def body(t, carry):
        for i in range(8):
            j = t * 8 + i
            q = staying[j]
            span_x[pl.ds(q * ROW, FIELDS), :] = x_rows[pl.ds(j * ROW, FIELDS), :]
            source = jnp.minimum(q, COLS - 1)
            block_inc[pl.ds(j * ROW, ROW), :] = inc_rows[pl.ds(source * ROW, ROW), :]
        return carry

    lax.fori_loop(0, COLS // 8, body, 0)


def tile_block(tiles, g, f):
    return jnp.concatenate(
        [tiles[pl.ds((g * 16 + i) * 48 + f * 8, 8), :] for i in range(16)], axis=0
    )


def row_block(rows, g, f):
    return jnp.concatenate(
        [rows[pl.ds((g * 128 + i * 8) * ROW + f, 8, stride=ROW), :] for i in range(16)], axis=0
    )


def transpose_in(load_x, load_inc, wind, right):
    def body(g, carry):
        for f in range(FIELDS):
            x = load_x(g, f)
            if f in RICHARDSON:
                wind[RICHARDSON[f], pl.ds(g * GROUP, LEV), :] = x.T
            right[f, pl.ds(g * GROUP, LEV), :] = (x + load_inc(g, f)).T
        return carry

    lax.fori_loop(0, 8, body, 0)


def transpose_out(right, tiles):
    def body(g, carry):
        for f in range(FIELDS):
            block = right[f, pl.ds(g * GROUP, LEV), :].T
            for i in range(16):
                tiles[pl.ds((g * 16 + i) * 48 + f * 8, 8), :] = block[i * 8 : (i + 1) * 8]
        return carry

    lax.fori_loop(0, 8, body, 0)


def level(ref, f, k):
    return ref[f, pl.ds(k, 8, stride=GROUP), :]


def put_level(ref, f, k, value):
    ref[f, pl.ds(k, 8, stride=GROUP), :] = value


def interface_weight(eddy, upper, lower):
    lapse = upper[0] - lower[0]
    u = upper[1] - lower[1]
    v = upper[2] - lower[2]
    shear = u * u + v * v + 0.1
    unstable = lapse < 0.0
    stable_root = shear + 10.0 * lapse
    top = jnp.where(unstable, shear - 8.0 * lapse, shear * shear)
    bottom = jnp.where(unstable, shear - lapse, stable_root * stable_root)
    wind = eddy * (top / bottom)
    return (1.35 * wind, wind)


def solve(wind, right, factor, forcing, eddy):
    for f in range(FIELDS):
        put_level(right, f, LEV - 1, level(right, f, LEV - 1) + forcing[f])

    def state(k):
        return [level(wind, i, k) for i in range(3)]

    zero = jnp.zeros((8, 128), jnp.float32)

    def eliminate(i, carry):
        excess, moved, above, below = carry
        ks = (i, LEV - 1 - i)
        inner = (state(i + 1), state(LEV - 2 - i))
        weights = (
            interface_weight(eddy, above, inner[0]),
            interface_weight(eddy, inner[1], below),
        )
        new_excess = [[], []]
        new_moved = [[], []]
        for side in range(2):
            ratio = []
            inverse = []
            for m in range(2):
                base = 1.0 + excess[side][m]
                inv = 1.0 / (base + weights[side][m])
                out = weights[side][m] * inv
                factor[side, m, i] = out
                ratio.append(out)
                inverse.append(inv)
                new_excess[side].append(base * out)
            for f in range(FIELDS):
                m = 0 if f in HEAT else 1
                z = level(right, f, ks[side]) + moved[side][f]
                put_level(right, f, ks[side], z * inverse[m])
                new_moved[side].append(z * ratio[m])
        return new_excess, new_moved, inner[0], inner[1]

    start = ([[zero] * 2] * 2, [[zero] * FIELDS] * 2, state(0), state(LEV - 1))
    half = LEV // 2
    excess, moved, above, below = lax.fori_loop(0, half - 1, eliminate, start, unroll=3)
    weight = interface_weight(eddy, above, below)
    solved = [[], []]
    for f in range(FIELDS):
        m = 0 if f in HEAT else 1
        w = weight[m]
        a = 1.0 + excess[0][m]
        b = 1.0 + excess[1][m]
        inv = 1.0 / (a * b + w * (a + b))
        za = level(right, f, half - 1) + moved[0][f]
        zb = level(right, f, half) + moved[1][f]
        ya = ((b + w) * za + w * zb) * inv
        yb = ((a + w) * zb + w * za) * inv
        put_level(right, f, half - 1, ya)
        put_level(right, f, half, yb)
        solved[0].append(ya)
        solved[1].append(yb)

    def substitute(i, carry):
        step = half - 2 - i
        ks = (step, LEV - 1 - step)
        new = [[], []]
        for side in range(2):
            ratio = [factor[side, m, step] for m in range(2)]
            for f in range(FIELDS):
                m = 0 if f in HEAT else 1
                y = level(right, f, ks[side]) + ratio[m] * carry[side][f]
                put_level(right, f, ks[side], y)
                new[side].append(y)
        return new

    lax.fori_loop(0, half - 1, substitute, solved, unroll=3)


def finish_kernel(
    departing, arriving, edges, x, inc, forcing, eddy, recv, span_rows, block_rows,
    span_out, block_out, left_rows, right_rows, wind, right, factor, scalars,
):
    def land(p, carry):
        for c in range(CAP):
            q = arriving[p * CAP + c]
            span_rows[pl.ds(q * ROW, FIELDS), :] = recv[pl.ds(p * MESSAGE + c * FIELDS, FIELDS), :]
        for c in range(CAP):
            j = departing[p * CAP + c]
            block_rows[pl.ds(j * ROW, ROW), :] = recv[pl.ds(p * MESSAGE + X_PART + c * ROW, ROW), :]
        return carry

    lax.fori_loop(0, PEERS, land, 0)

    transpose_in(
        lambda g, f: tile_block(x, g, f), lambda g, f: row_block(block_rows, g, f), wind, right
    )
    for g in range(8):
        scalars[0, pl.ds(g * GROUP, LEV), :] = row_block(block_rows, g, FIELDS).T
    solve(
        wind, right, factor,
        [level(scalars, 0, f) for f in range(FIELDS)],
        level(scalars, 0, FIELDS),
    )
    transpose_out(right, block_out)

    def edge(k, carry):
        for side, out in ((0, left_rows), (1, right_rows)):
            j = edges[side * EDGE + k]
            base = (j >> 3) * 48 + (j & 7)
            out[pl.ds(k * FIELDS, FIELDS), :] = block_out[pl.ds(base, FIELDS, stride=8), :]
        return carry

    lax.fori_loop(0, EDGE, edge, 0, unroll=4)

    transpose_in(
        lambda g, f: row_block(span_rows, g, f), lambda g, f: tile_block(inc, g, f), wind, right
    )
    solve(wind, right, factor, [forcing[f] for f in range(FIELDS)], eddy[...])
    transpose_out(right, span_out)


def average_kernel(edges, column, own_left, own_right, far_left, far_right, out):
    out[...] = column[...]

    def body(k, carry):
        for side, own, far in ((0, own_left, far_left), (1, own_right, far_right)):
            j = edges[side * EDGE + k]
            base = (j >> 3) * 48 + (j & 7)
            rows = pl.ds(k * FIELDS, FIELDS)
            out[pl.ds(base, FIELDS, stride=8), :] = (own[rows, :] + far[rows, :]) * 0.5
        return carry

    lax.fori_loop(0, EDGE, body, 0, unroll=4)


def shape(*dims):
    return jax.ShapeDtypeStruct(dims, jnp.float32)


def in_smem():
    return pl.BlockSpec(memory_space=pltpu.SMEM)


def in_vmem():
    return pl.BlockSpec(memory_space=pltpu.VMEM)


def call(kernel, tables, arrays, out_shape, scratch=(), aliases={}, cost=None):
    return pl.pallas_call(
        kernel,
        out_shape=out_shape,
        in_specs=[in_smem()] * len(tables) + [in_vmem()] * len(arrays),
        out_specs=jax.tree.map(lambda _: in_vmem(), out_shape),
        scratch_shapes=list(scratch),
        input_output_aliases=aliases,
        compiler_params=pltpu.CompilerParams(vmem_limit_bytes=VMEM_LIMIT),
        cost_estimate=cost,
    )(*tables, *arrays)


def on_device(
    dynamics_profile_values,
    parameterized_increments,
    ground_exchange_rates,
    sunlit_indicator,
    eddy_coefficient_scale,
    departing_profile_indices,
    arriving_parcel_places,
    resident_parcel_place,
    boundary_profile_indices,
):
    departing = departing_profile_indices.reshape(-1)
    arriving = arriving_parcel_places.reshape(-1)
    staying = resident_parcel_place.reshape(-1)
    edges = boundary_profile_indices.reshape(-1)
    x = to_tiles(dynamics_profile_values)
    inc = to_tiles(parameterized_increments)
    forcing = ground_exchange_rates * (0.5 + sunlit_indicator.astype(jnp.float32))
    eddy = eddy_coefficient_scale
    scalars = jnp.concatenate([forcing, eddy[None], eddy[None]], axis=0)
    rows = pltpu.VMEM((ROWS_ALLOC, LEV), jnp.float32)

    send = call(
        pack_kernel, (departing, arriving), (x, inc, scalars),
        shape(PEERS * MESSAGE, LEV), (rows, rows),
    )
    recv = lax.all_to_all(
        send.reshape(PEERS, MESSAGE, LEV), ("blk", "sub"), split_axis=0, concat_axis=0, tiled=True
    ).reshape(PEERS * MESSAGE, LEV)
    span_rows, block_rows = call(
        resident_kernel, (staying,), (x, inc, scalars),
        (shape(ROWS_ALLOC, LEV), shape(ROWS_ALLOC, LEV)), (rows, rows),
        cost=pl.CostEstimate(flops=0, bytes_accessed=14 * 2**20, transcendentals=0),
    )
    transposed = functools.partial(pltpu.VMEM, dtype=jnp.float32)
    span_out, block_out, left_rows, right_rows = call(
        finish_kernel, (departing, arriving, edges),
        (x, inc, forcing.reshape(FIELDS, 8, LEV), eddy.reshape(8, LEV), recv, span_rows, block_rows),
        (shape(COLS * FIELDS, LEV), shape(COLS * FIELDS, LEV), shape(EDGE * FIELDS, LEV), shape(EDGE * FIELDS, LEV)),
        (
            transposed((3, 8 * GROUP, LEV)),
            transposed((FIELDS, 8 * GROUP, LEV)),
            transposed((2, 2, LEV // 2, 8, LEV)),
            transposed((1, 8 * GROUP, LEV)),
        ),
    )
    count = lax.axis_size("blk")
    far_left = lax.ppermute(right_rows, "blk", [(i, (i + 1) % count) for i in range(count)])
    far_right = lax.ppermute(left_rows, "blk", [((i + 1) % count, i) for i in range(count)])
    column = call(
        average_kernel, (edges,), (block_out, left_rows, right_rows, far_left, far_right),
        shape(COLS * FIELDS, LEV),
    )
    return from_tiles(span_out), from_tiles(column)


def solution(mesh):
    one = P(("blk", "sub"))
    placed = (one, one, P(None, ("blk", "sub")), one, one, one, one, one, one)
    return jax.shard_map(
        on_device, mesh=mesh, in_specs=placed, out_specs=(one, one), check_vma=False
    )
```

```python
import jax
import jax.numpy as jnp
from jax import lax
from jax.experimental import pallas as pl
from jax.experimental.pallas import tpu as pltpu
from jax.sharding import PartitionSpec as P

FIELDS = 6
LEV = 128
COLS = 1024
PEERS = 128
CAP = 8
EDGE = 128
ROW = 7
DUMP = COLS
ROWS_ALLOC = 7176
X_PART = CAP * FIELDS
MESSAGE = X_PART + CAP * ROW
GROUP = 137
VMEM_LIMIT = 60 * 2**20
HEAT = (0, 1, 4, 5)
RICHARDSON = {0: 0, 2: 1, 3: 2}


def to_tiles(rows):
    return rows.reshape(COLS // 8, 8, FIELDS, LEV).transpose(0, 2, 1, 3).reshape(COLS * FIELDS, LEV)


def from_tiles(tiles):
    return tiles.reshape(COLS // 8, FIELDS, 8, LEV).transpose(0, 2, 1, 3).reshape(COLS, FIELDS * LEV)


def copy_chunks(pairs, sems, first):
    copies = [
        pltpu.make_async_copy(source, target, sems.at[first + i])
        for i, (source, target) in enumerate(pairs)
    ]
    for one in copies:
        one.start()
    return copies


def chunked(source, target, parts):
    size = source.shape[0] // parts
    return [
        (source.at[pl.ds(i * size, size)], target.at[pl.ds(i * size, size)]) for i in range(parts)
    ]


def spread_rows(tiles, rows, first, count):
    def body(t, carry):
        for f in range(FIELDS):
            rows[pl.ds(t * 8 * ROW + f, 8, stride=ROW), :] = tiles[pl.ds(t * 48 + f * 8, 8), :]
        return carry

    lax.fori_loop(first, first + count, body, 0, unroll=4)


def spread_scalars(rates, sunlit, eddy, rows):
    for g in range(8):
        lanes = pl.ds(g * 128, 128)
        one = pl.ds(g, 1)
        forcing = rates[:, lanes] * (0.5 + sunlit[one, :].astype(jnp.float32))
        part = jnp.concatenate([forcing, eddy[one, :], eddy[one, :]], axis=0)
        square = jnp.concatenate([part] * 16, axis=0).T
        for i in range(16):
            rows[pl.ds((g * 128 + i * 8) * ROW + FIELDS, 8, stride=ROW), :] = square[i * 8 : (i + 1) * 8]


def load_rows(x, inc, rates, sunlit, eddy, x_tiles, inc_tiles, x_rows, inc_rows, sems):
    parts = 4
    x_copies = copy_chunks(chunked(x, x_tiles, parts), sems, 0)
    inc_copies = copy_chunks(chunked(inc, inc_tiles, parts), sems, parts)
    spread_scalars(rates, sunlit, eddy, inc_rows)
    count = COLS // 8 // parts
    for copies, tiles, rows in ((x_copies, x_tiles, x_rows), (inc_copies, inc_tiles, inc_rows)):
        for i, one in enumerate(copies):
            one.wait()
            spread_rows(tiles, rows, i * count, count)


def pack_kernel(
    departing, arriving, x, inc, rates, sunlit, eddy, send,
    x_tiles, inc_tiles, x_rows, inc_rows, packed, sems,
):
    load_rows(x, inc, rates, sunlit, eddy, x_tiles, inc_tiles, x_rows, inc_rows, sems)

    def body(p, carry):
        for c in range(CAP):
            j = jnp.minimum(departing[c, p], COLS - 1)
            packed[pl.ds(p * MESSAGE + c * FIELDS, FIELDS), :] = x_rows[pl.ds(j * ROW, FIELDS), :]
        for c in range(CAP):
            q = jnp.minimum(arriving[c, p], COLS - 1)
            packed[pl.ds(p * MESSAGE + X_PART + c * ROW, ROW), :] = inc_rows[pl.ds(q * ROW, ROW), :]
        return carry

    parts = 8
    step = PEERS // parts
    copies = []
    for i, pair in enumerate(chunked(packed, send, parts)):
        lax.fori_loop(i * step, (i + 1) * step, body, 0)
        copies += copy_chunks([pair], sems, i)
    for one in copies:
        one.wait()


def resident_kernel(
    staying, x, inc, rates, sunlit, eddy, span_x, block_inc,
    x_tiles, inc_tiles, x_rows, inc_rows, sems,
):
    load_rows(x, inc, rates, sunlit, eddy, x_tiles, inc_tiles, x_rows, inc_rows, sems)

    def body(t, carry):
        for i in range(8):
            j = t * 8 + i
            q = staying[j]
            span_x[pl.ds(q * ROW, FIELDS), :] = x_rows[pl.ds(j * ROW, FIELDS), :]
            source = jnp.minimum(q, COLS - 1)
            block_inc[pl.ds(j * ROW, ROW), :] = inc_rows[pl.ds(source * ROW, ROW), :]
        return carry

    lax.fori_loop(0, COLS // 8, body, 0)


def tile_block(tiles, g, f):
    return jnp.concatenate(
        [tiles[pl.ds((g * 16 + i) * 48 + f * 8, 8), :] for i in range(16)], axis=0
    )


def row_block(rows, g, f):
    return jnp.concatenate(
        [rows[pl.ds((g * 128 + i * 8) * ROW + f, 8, stride=ROW), :] for i in range(16)], axis=0
    )


def transpose_in(load_x, load_inc, wind, right):
    def body(g, carry):
        for f in range(FIELDS):
            x = load_x(g, f)
            if f in RICHARDSON:
                wind[RICHARDSON[f], pl.ds(g * GROUP, LEV), :] = x.T
            right[f, pl.ds(g * GROUP, LEV), :] = (x + load_inc(g, f)).T
        return carry

    lax.fori_loop(0, 8, body, 0)


def transpose_out(right, tiles, out, sems):
    copies = []
    for g, pair in enumerate(chunked(tiles, out, 8)):
        def body(f, carry):
            block = right[f, pl.ds(g * GROUP, LEV), :].T
            for i in range(16):
                tiles[pl.ds((g * 16 + i) * 48 + f * 8, 8), :] = block[i * 8 : (i + 1) * 8]
            return carry

        lax.fori_loop(0, FIELDS, body, 0, unroll=True)
        copies += copy_chunks([pair], sems, g)
    return copies


def level(ref, f, k):
    return ref[f, pl.ds(k, 8, stride=GROUP), :]


def put_level(ref, f, k, value):
    ref[f, pl.ds(k, 8, stride=GROUP), :] = value


def interface_weight(eddy, upper, lower):
    lapse = upper[0] - lower[0]
    u = upper[1] - lower[1]
    v = upper[2] - lower[2]
    shear = u * u + v * v + 0.1
    unstable = lapse < 0.0
    stable_root = shear + 10.0 * lapse
    top = jnp.where(unstable, shear - 8.0 * lapse, shear * shear)
    bottom = jnp.where(unstable, shear - lapse, stable_root * stable_root)
    wind = eddy * (top / bottom)
    return (1.35 * wind, wind)


def solve(wind, right, factor, forcing, eddy):
    for f in range(FIELDS):
        put_level(right, f, LEV - 1, level(right, f, LEV - 1) + forcing[f])

    def state(k):
        return [level(wind, i, k) for i in range(3)]

    zero = jnp.zeros((8, 128), jnp.float32)

    def eliminate(i, carry):
        excess, moved, above, below = carry
        ks = (i, LEV - 1 - i)
        inner = (state(i + 1), state(LEV - 2 - i))
        weights = (
            interface_weight(eddy, above, inner[0]),
            interface_weight(eddy, inner[1], below),
        )
        new_excess = [[], []]
        new_moved = [[], []]
        for side in range(2):
            ratio = []
            inverse = []
            for m in range(2):
                base = 1.0 + excess[side][m]
                inv = 1.0 / (base + weights[side][m])
                out = weights[side][m] * inv
                factor[side, m, i] = out
                ratio.append(out)
                inverse.append(inv)
                new_excess[side].append(base * out)
            for f in range(FIELDS):
                m = 0 if f in HEAT else 1
                z = level(right, f, ks[side]) + moved[side][f]
                put_level(right, f, ks[side], z * inverse[m])
                new_moved[side].append(z * ratio[m])
        return new_excess, new_moved, inner[0], inner[1]

    start = ([[zero] * 2] * 2, [[zero] * FIELDS] * 2, state(0), state(LEV - 1))
    half = LEV // 2
    excess, moved, above, below = lax.fori_loop(0, half - 1, eliminate, start, unroll=3)
    weight = interface_weight(eddy, above, below)
    solved = [[], []]
    for f in range(FIELDS):
        m = 0 if f in HEAT else 1
        w = weight[m]
        a = 1.0 + excess[0][m]
        b = 1.0 + excess[1][m]
        inv = 1.0 / (a * b + w * (a + b))
        za = level(right, f, half - 1) + moved[0][f]
        zb = level(right, f, half) + moved[1][f]
        ya = ((b + w) * za + w * zb) * inv
        yb = ((a + w) * zb + w * za) * inv
        put_level(right, f, half - 1, ya)
        put_level(right, f, half, yb)
        solved[0].append(ya)
        solved[1].append(yb)

    def substitute(i, carry):
        step = half - 2 - i
        ks = (step, LEV - 1 - step)
        new = [[], []]
        for side in range(2):
            ratio = [factor[side, m, step] for m in range(2)]
            for f in range(FIELDS):
                m = 0 if f in HEAT else 1
                y = level(right, f, ks[side]) + ratio[m] * carry[side][f]
                put_level(right, f, ks[side], y)
                new[side].append(y)
        return new

    lax.fori_loop(0, half - 1, substitute, solved, unroll=3)


def land(recv_copies, place, put):
    step = PEERS // len(recv_copies)

    def body(p, carry):
        for c in range(CAP):
            put(p, c, place[c, p])
        return carry

    for i, one in enumerate(recv_copies):
        one.wait()
        lax.fori_loop(i * step, (i + 1) * step, body, 0)


def start_landing(rows, rows_in, recv, landed, offset, other, tiles, sems):
    size = landed.shape[1]
    parts = 8
    step = PEERS // parts
    first = copy_chunks([(rows_in, rows)], sems, 0)
    arrivals = copy_chunks(
        [
            (recv.at[pl.ds(i * step, step), pl.ds(offset, size), :], landed.at[pl.ds(i * step, step)])
            for i in range(parts)
        ],
        sems, 1,
    )
    last = copy_chunks([(other, tiles)], sems, 1 + parts)
    first[0].wait()
    return arrivals, last[0]


def block_kernel(
    departing, edges, x, rows_in, recv, out, left_rows, right_rows,
    tiles, rows, landed, wind, right, factor, scalars, sems,
):
    arrivals, last = start_landing(rows, rows_in, recv, landed, X_PART, x, tiles, sems)

    def put(p, c, j):
        rows[pl.ds(j * ROW, ROW), :] = landed[p, pl.ds(c * ROW, ROW), :]

    land(arrivals, departing, put)
    last.wait()
    transpose_in(
        lambda g, f: tile_block(tiles, g, f), lambda g, f: row_block(rows, g, f), wind, right
    )
    for g in range(8):
        scalars[0, pl.ds(g * GROUP, LEV), :] = row_block(rows, g, FIELDS).T
    solve(
        wind, right, factor,
        [level(scalars, 0, f) for f in range(FIELDS)],
        level(scalars, 0, FIELDS),
    )
    copies = transpose_out(right, tiles, out, sems)

    def edge(k, carry):
        for side, edge_out in ((0, left_rows), (1, right_rows)):
            j = edges[side, k]
            base = (j >> 3) * 48 + (j & 7)
            edge_out[pl.ds(k * FIELDS, FIELDS), :] = tiles[pl.ds(base, FIELDS, stride=8), :]
        return carry

    lax.fori_loop(0, EDGE, edge, 0, unroll=4)
    for one in copies:
        one.wait()


def span_kernel(
    arriving, inc, rates, sunlit, eddy, rows_in, recv, out,
    tiles, rows, landed, wind, right, factor, sems,
):
    arrivals, last = start_landing(rows, rows_in, recv, landed, 0, inc, tiles, sems)

    def put(p, c, q):
        rows[pl.ds(q * ROW, FIELDS), :] = landed[p, pl.ds(c * FIELDS, FIELDS), :]

    land(arrivals, arriving, put)
    last.wait()
    transpose_in(
        lambda g, f: row_block(rows, g, f), lambda g, f: tile_block(tiles, g, f), wind, right
    )
    lit = 0.5 + sunlit[...].astype(jnp.float32)
    forcing = [
        jnp.concatenate([rates[pl.ds(f, 1), pl.ds(g * 128, 128)] for g in range(8)], axis=0) * lit
        for f in range(FIELDS)
    ]
    solve(wind, right, factor, forcing, eddy[...])
    for one in transpose_out(right, tiles, out, sems):
        one.wait()


def average_kernel(edges, column, own_left, own_right, far_left, far_right, out, buf, sides, sems):
    load = copy_chunks([(column, buf)], sems, 0)
    load += copy_chunks(
        [(one, sides.at[i]) for i, one in enumerate((own_left, own_right, far_left, far_right))],
        sems, 1,
    )
    for one in load:
        one.wait()

    def body(k, carry):
        for side in range(2):
            j = edges[side, k]
            base = (j >> 3) * 48 + (j & 7)
            rows = pl.ds(k * FIELDS, FIELDS)
            buf[pl.ds(base, FIELDS, stride=8), :] = (sides[side, rows, :] + sides[2 + side, rows, :]) * 0.5
        return carry

    lax.fori_loop(0, EDGE, body, 0, unroll=4)
    for one in copy_chunks(chunked(buf, out, 4), sems, 0):
        one.wait()


def shape(*dims):
    return jax.ShapeDtypeStruct(dims, jnp.float32)


def spec(space):
    return pl.BlockSpec(memory_space=space)


def call(kernel, operands, outputs, scratch, sem_count, cost=None):
    return pl.pallas_call(
        kernel,
        out_shape=tuple(one for _, one in outputs),
        in_specs=[spec(space) for space, _ in operands],
        out_specs=tuple(spec(space) for space, _ in outputs),
        scratch_shapes=[
            *(pltpu.VMEM(dims, jnp.float32) for dims in scratch),
            pltpu.SemaphoreType.DMA((sem_count,)),
        ],
        compiler_params=pltpu.CompilerParams(vmem_limit_bytes=VMEM_LIMIT),
        cost_estimate=cost,
    )(*(array for _, array in operands))


def on_device(
    dynamics_profile_values,
    parameterized_increments,
    ground_exchange_rates,
    sunlit_indicator,
    eddy_coefficient_scale,
    departing_profile_indices,
    arriving_parcel_places,
    resident_parcel_place,
    boundary_profile_indices,
):
    smem, vmem, hbm = pltpu.SMEM, pltpu.VMEM, pl.ANY
    departing = (smem, departing_profile_indices[0].T)
    arriving = (smem, arriving_parcel_places[0].T)
    staying = (smem, resident_parcel_place.reshape(-1))
    edges = (smem, boundary_profile_indices[0])
    x = (hbm, to_tiles(dynamics_profile_values))
    inc = (hbm, to_tiles(parameterized_increments))
    physics = (
        (vmem, ground_exchange_rates),
        (vmem, sunlit_indicator.reshape(8, LEV)),
        (vmem, eddy_coefficient_scale.reshape(8, LEV)),
    )
    whole = (COLS * FIELDS, LEV)
    rows = (ROWS_ALLOC, LEV)
    side = (EDGE * FIELDS, LEV)
    transposed = ((3, 8 * GROUP, LEV), (FIELDS, 8 * GROUP, LEV), (2, 2, LEV // 2, 8, LEV))

    (send,) = call(
        pack_kernel, (departing, arriving, x, inc, *physics), ((hbm, shape(PEERS * MESSAGE, LEV)),),
        (whole, whole, rows, rows, (PEERS * MESSAGE, LEV)), 8,
    )
    recv = lax.all_to_all(
        send.reshape(PEERS, MESSAGE, LEV), ("blk", "sub"), split_axis=0, concat_axis=0, tiled=True
    )
    span_rows, block_rows = call(
        resident_kernel, (staying, x, inc, *physics), ((vmem, shape(*rows)), (vmem, shape(*rows))),
        (whole, whole, rows, rows), 8,
        pl.CostEstimate(flops=0, bytes_accessed=14 * 2**20, transcendentals=0),
    )
    column, left_rows, right_rows = call(
        block_kernel, (departing, edges, x, (hbm, block_rows), (hbm, recv)),
        ((hbm, shape(*whole)), (vmem, shape(*side)), (vmem, shape(*side))),
        (whole, rows, (PEERS, CAP * ROW, LEV), *transposed, (1, 8 * GROUP, LEV)), 10,
    )
    count = lax.axis_size("blk")
    far_left = lax.ppermute(right_rows, "blk", [(i, (i + 1) % count) for i in range(count)])
    far_right = lax.ppermute(left_rows, "blk", [((i + 1) % count, i) for i in range(count)])
    (span_out,) = call(
        span_kernel, (arriving, inc, *physics, (hbm, span_rows), (hbm, recv)),
        ((hbm, shape(*whole)),),
        (whole, rows, (PEERS, X_PART, LEV), *transposed), 10,
        pl.CostEstimate(flops=10**9, bytes_accessed=20 * 2**20, transcendentals=0),
    )
    (column,) = call(
        average_kernel,
        (edges, *((hbm, one) for one in (column, left_rows, right_rows, far_left, far_right))),
        ((hbm, shape(*whole)),),
        (whole, (4, *side)), 5,
    )
    return from_tiles(span_out), from_tiles(column)


def solution(mesh):
    one = P(("blk", "sub"))
    placed = (one, one, P(None, ("blk", "sub")), one, one, one, one, one, one)
    return jax.shard_map(
        on_device, mesh=mesh, in_specs=placed, out_specs=(one, one), check_vma=False
    )
```

```python
import jax
import jax.numpy as jnp
from jax import lax
from jax.experimental import pallas as pl
from jax.experimental.pallas import tpu as pltpu
from jax.sharding import PartitionSpec as P

FIELDS = 6
LEV = 128
COLS = 1024
PEERS = 128
CAP = 8
EDGE = 128
ROW = 7
DUMP = COLS
ROWS_ALLOC = 7176
SLOTS = 11
SCALARS_AT = SLOTS * FIELDS
MESSAGE = 72
HOP = 8
RESENT = CAP * FIELDS
SPARE = PEERS * MESSAGE
PACKED = SPARE + 8
LANDED = SPARE + 32
PLAN = 256
PLAN_COUNT = 128
PLAN_FAILED = 129
GROUP = 137
VMEM_LIMIT = 60 * 2**20
HEAT = (0, 1, 4, 5)
RICHARDSON = {0: 0, 2: 1, 3: 2}


def to_tiles(rows):
    return rows.reshape(COLS // 8, 8, FIELDS, LEV).transpose(0, 2, 1, 3).reshape(COLS * FIELDS, LEV)


def from_tiles(tiles):
    return tiles.reshape(COLS // 8, FIELDS, 8, LEV).transpose(0, 2, 1, 3).reshape(COLS, FIELDS * LEV)


def copy_chunks(pairs, sems, first):
    copies = [
        pltpu.make_async_copy(source, target, sems.at[first + i])
        for i, (source, target) in enumerate(pairs)
    ]
    for one in copies:
        one.start()
    return copies


def chunked(source, target, parts):
    size = source.shape[0] // parts
    return [
        (source.at[pl.ds(i * size, size)], target.at[pl.ds(i * size, size)]) for i in range(parts)
    ]


def spread_rows(tiles, rows, first, count):
    def body(t, carry):
        for f in range(FIELDS):
            rows[pl.ds(t * 8 * ROW + f, 8, stride=ROW), :] = tiles[pl.ds(t * 48 + f * 8, 8), :]
        return carry

    lax.fori_loop(first, first + count, body, 0, unroll=4)


def spread_scalars(rates, sunlit, eddy, rows):
    for g in range(8):
        lanes = pl.ds(g * 128, 128)
        one = pl.ds(g, 1)
        forcing = rates[:, lanes] * (0.5 + sunlit[one, :].astype(jnp.float32))
        part = jnp.concatenate([forcing, eddy[one, :], eddy[one, :]], axis=0)
        square = jnp.concatenate([part] * 16, axis=0).T
        for i in range(16):
            rows[pl.ds((g * 128 + i * 8) * ROW + FIELDS, 8, stride=ROW), :] = square[i * 8 : (i + 1) * 8]


def load_rows(x, inc, rates, sunlit, eddy, x_tiles, inc_tiles, x_rows, inc_rows, sems):
    parts = 4
    x_copies = copy_chunks(chunked(x, x_tiles, parts), sems, 0)
    inc_copies = copy_chunks(chunked(inc, inc_tiles, parts), sems, parts)
    spread_scalars(rates, sunlit, eddy, inc_rows)
    count = COLS // 8 // parts
    for copies, tiles, rows in ((x_copies, x_tiles, x_rows), (inc_copies, inc_tiles, inc_rows)):
        for i, one in enumerate(copies):
            one.wait()
            spread_rows(tiles, rows, i * count, count)


def device_index():
    return lax.axis_index("blk") * lax.axis_size("sub") + lax.axis_index("sub")


def wrap(index):
    return index & (PEERS - 1)


def fold(offset):
    return jnp.minimum(offset, PEERS - offset)


def fill_tables(departing, arriving, tables, info):
    out_places = departing[...]
    in_places = arriving[...]
    slot = lax.broadcasted_iota(jnp.int32, (CAP, PEERS), 0)
    peer = lax.broadcasted_iota(jnp.int32, (CAP, PEERS), 1)
    leaving = jnp.sum((out_places < COLS).astype(jnp.int32), axis=0, keepdims=True)
    coming = jnp.sum((in_places < COLS).astype(jnp.int32), axis=0, keepdims=True)
    base = peer * MESSAGE
    place = coming + slot
    tables[0:8] = jnp.minimum(out_places, COLS - 1) * ROW
    tables[8:16] = jnp.where(
        (slot < leaving) & (place < SLOTS), base + place * FIELDS, SPARE
    )
    tables[16:24] = jnp.minimum(in_places, COLS - 1) * ROW
    tables[24:32] = jnp.where(slot < coming, base + slot * FIELDS, SPARE)
    counts = jnp.where(slot == 0, leaving, coming)
    tables[32:40] = counts
    info[...] = counts


def make_plan(me, counts, plan, fill, used):
    def start(o, carry):
        p = wrap(me + o)
        fill[o] = jnp.minimum(counts(0, p) + counts(1, p), SLOTS)
        used[o] = 0
        return carry

    lax.fori_loop(1, PEERS // 2, start, 0)
    for o in (0, PEERS // 2):
        fill[o] = SLOTS
        used[o] = 1

    def offset(o, carry):
        p = wrap(me + o)
        leaving = counts(0, p)
        coming = counts(1, p)
        excess = jnp.maximum(leaving + coming - SLOTS, 0)
        middle = o == PEERS // 2

        def column(t, carry):
            last, count, failed = carry

            def search(state):
                tries, u, _ = state
                u = jnp.where(u == PEERS - 1, 1, u + 1)
                taken = (fill[fold(u)] >= SLOTS) | (used[fold(wrap(o - u))] > 0)
                return tries + 1, u, taken

            tries, u, taken = lax.while_loop(
                lambda state: state[2] & (state[0] < PEERS), search,
                (jnp.int32(0), last, jnp.bool_(True)),
            )
            found = jnp.logical_not(taken)
            r = fill[fold(u)]
            slot = leaving - excess + jnp.where(middle, 2 * t, t)
            mirror_slot = jnp.where(middle, slot + 1, coming - excess + t)
            both = jnp.logical_not(middle) | (2 * t + 1 < excess)

            @pl.when(found)
            def _():
                fill[fold(u)] = r + 1
                used[fold(wrap(o - u))] = 1
                plan[count] = o | (u << 7) | (r << 14) | (slot << 18)
                plan[count + 1] = (PEERS - o) | ((PEERS - u) << 7) | (r << 14) | (mirror_slot << 18)

            count = count + jnp.where(found, jnp.where(both, 2, 1), 0)
            return u, count, failed | taken.astype(jnp.int32)

        rounds = jnp.where(middle, (excess + 1) >> 1, excess)
        return lax.fori_loop(0, rounds, column, carry)

    zero = jnp.int32(0)
    _, count, failed = lax.fori_loop(1, PEERS // 2 + 1, offset, (zero, zero, zero))
    plan[PLAN_COUNT] = count
    plan[PLAN_FAILED] = failed


def planned(plan, i):
    entry = plan[i]
    o = entry & 127
    u = (entry >> 7) & 127
    return o, u, (entry >> 14) & 15, (entry >> 18) & 15


def pack_kernel(
    departing, arriving, x, inc, rates, sunlit, eddy, send, plan, info,
    x_tiles, inc_tiles, x_rows, inc_rows, packed, tables, places, fill, used, sems, table_sem,
):
    parts = 4
    x_copies = copy_chunks(chunked(x, x_tiles, parts), sems, 0)
    inc_copies = copy_chunks(chunked(inc, inc_tiles, parts), sems, parts)
    fill_tables(departing, arriving, tables, info)
    move = pltpu.make_async_copy(tables, places, table_sem.at[0])
    move.start()
    spread_scalars(rates, sunlit, eddy, inc_rows)
    move.wait()
    me = device_index()
    make_plan(me, lambda row, p: places[32 + row, p], plan, fill, used)
    count = COLS // 8 // parts
    for copies, tiles, rows in ((x_copies, x_tiles, x_rows), (inc_copies, inc_tiles, inc_rows)):
        for i, one in enumerate(copies):
            one.wait()
            spread_rows(tiles, rows, i * count, count)

    def relay(i, carry):
        o, u, r, c = planned(plan, i)
        source = places[c, wrap(me + o)]
        target = wrap(me + u) * MESSAGE + r * FIELDS
        packed[pl.ds(target, FIELDS), :] = x_rows[pl.ds(source, FIELDS), :]
        return carry

    lax.fori_loop(0, plan[PLAN_COUNT], relay, 0)
    group = lax.broadcasted_iota(jnp.int32, (1, LEV), 1) >> 3

    def body(p, carry):
        scalars = jnp.zeros((1, LEV), jnp.float32)
        for c in range(CAP):
            packed[pl.ds(places[8 + c, p], FIELDS), :] = x_rows[pl.ds(places[c, p], FIELDS), :]
            row = places[16 + c, p]
            packed[pl.ds(places[24 + c, p], FIELDS), :] = inc_rows[pl.ds(row, FIELDS), :]
            scalars = jnp.where(group == c, inc_rows[pl.ds(row + FIELDS, 1), :], scalars)
        packed[pl.ds(p * MESSAGE + SCALARS_AT, 1), :] = scalars
        return carry

    parts = 8
    step = PEERS // parts
    size = step * MESSAGE
    copies = []
    for i in range(parts):
        lax.fori_loop(i * step, (i + 1) * step, body, 0)
        part = pl.ds(i * size, size)
        copies += copy_chunks([(packed.at[part], send.at[part])], sems, i)
    for one in copies:
        one.wait()


def relay_kernel(plan, recv, prepared, send, windows, sems):
    del prepared
    me = device_index()
    count = plan[PLAN_COUNT]

    def window(i):
        o, u, r, _ = planned(plan, i)
        row = r * FIELDS
        first = pl.multiple_of((row >> 3) << 3, 8)
        copy = pltpu.make_async_copy(
            recv.at[wrap(me - u), pl.ds(first, 16), :], windows.at[i], sems.at[i]
        )
        return copy, row - first, wrap(me + o - u)

    def fetch(i, carry):
        window(i)[0].start()
        return carry

    def forward(i, carry):
        copy, at, peer = window(i)
        copy.wait()
        send[pl.ds(peer * HOP, FIELDS), :] = windows[i, pl.ds(at, FIELDS), :]
        return carry

    lax.fori_loop(0, count, fetch, 0)
    lax.fori_loop(0, count, forward, 0)


def resend_kernel(departing, x, send, x_tiles, x_rows, packed, sems):
    (copy,) = copy_chunks([(x, x_tiles)], sems, 0)
    copy.wait()
    spread_rows(x_tiles, x_rows, 0, COLS // 8)

    def body(p, carry):
        for c in range(CAP):
            j = jnp.minimum(departing[c, p], COLS - 1)
            packed[pl.ds(p * RESENT + c * FIELDS, FIELDS), :] = x_rows[pl.ds(j * ROW, FIELDS), :]
        return carry

    lax.fori_loop(0, PEERS, body, 0)
    (copy,) = copy_chunks([(packed, send)], sems, 0)
    copy.wait()


def resident_kernel(
    staying, x, inc, rates, sunlit, eddy, span_x, block_inc,
    x_tiles, inc_tiles, x_rows, inc_rows, sems,
):
    load_rows(x, inc, rates, sunlit, eddy, x_tiles, inc_tiles, x_rows, inc_rows, sems)

    def body(t, carry):
        for i in range(8):
            j = t * 8 + i
            q = staying[j]
            span_x[pl.ds(q * ROW, FIELDS), :] = x_rows[pl.ds(j * ROW, FIELDS), :]
            source = jnp.minimum(q, COLS - 1)
            block_inc[pl.ds(j * ROW, ROW), :] = inc_rows[pl.ds(source * ROW, ROW), :]
        return carry

    lax.fori_loop(0, COLS // 8, body, 0)


def tile_block(tiles, g, f):
    return jnp.concatenate(
        [tiles[pl.ds((g * 16 + i) * 48 + f * 8, 8), :] for i in range(16)], axis=0
    )


def row_block(rows, g, f):
    return jnp.concatenate(
        [rows[pl.ds((g * 128 + i * 8) * ROW + f, 8, stride=ROW), :] for i in range(16)], axis=0
    )


def transpose_in(load_x, load_inc, wind, right):
    def body(g, carry):
        for f in range(FIELDS):
            x = load_x(g, f)
            if f in RICHARDSON:
                wind[RICHARDSON[f], pl.ds(g * GROUP, LEV), :] = x.T
            right[f, pl.ds(g * GROUP, LEV), :] = (x + load_inc(g, f)).T
        return carry

    lax.fori_loop(0, 8, body, 0)


def transpose_out(right, tiles, out, sems):
    copies = []
    for g, pair in enumerate(chunked(tiles, out, 8)):
        def body(f, carry):
            block = right[f, pl.ds(g * GROUP, LEV), :].T
            for i in range(16):
                tiles[pl.ds((g * 16 + i) * 48 + f * 8, 8), :] = block[i * 8 : (i + 1) * 8]
            return carry

        lax.fori_loop(0, FIELDS, body, 0, unroll=True)
        copies += copy_chunks([pair], sems, g)
    return copies


def level(ref, f, k):
    return ref[f, pl.ds(k, 8, stride=GROUP), :]


def put_level(ref, f, k, value):
    ref[f, pl.ds(k, 8, stride=GROUP), :] = value


def interface_weight(eddy, upper, lower):
    lapse = upper[0] - lower[0]
    u = upper[1] - lower[1]
    v = upper[2] - lower[2]
    shear = u * u + v * v + 0.1
    unstable = lapse < 0.0
    stable_root = shear + 10.0 * lapse
    top = jnp.where(unstable, shear - 8.0 * lapse, shear * shear)
    bottom = jnp.where(unstable, shear - lapse, stable_root * stable_root)
    wind = eddy * (top / bottom)
    return (1.35 * wind, wind)


def solve(wind, right, factor, forcing, eddy):
    for f in range(FIELDS):
        put_level(right, f, LEV - 1, level(right, f, LEV - 1) + forcing[f])

    def state(k):
        return [level(wind, i, k) for i in range(3)]

    zero = jnp.zeros((8, 128), jnp.float32)

    def eliminate(i, carry):
        excess, moved, above, below = carry
        ks = (i, LEV - 1 - i)
        inner = (state(i + 1), state(LEV - 2 - i))
        weights = (
            interface_weight(eddy, above, inner[0]),
            interface_weight(eddy, inner[1], below),
        )
        new_excess = [[], []]
        new_moved = [[], []]
        for side in range(2):
            ratio = []
            inverse = []
            for m in range(2):
                base = 1.0 + excess[side][m]
                inv = 1.0 / (base + weights[side][m])
                out = weights[side][m] * inv
                factor[side, m, i] = out
                ratio.append(out)
                inverse.append(inv)
                new_excess[side].append(base * out)
            for f in range(FIELDS):
                m = 0 if f in HEAT else 1
                z = level(right, f, ks[side]) + moved[side][f]
                put_level(right, f, ks[side], z * inverse[m])
                new_moved[side].append(z * ratio[m])
        return new_excess, new_moved, inner[0], inner[1]

    start = ([[zero] * 2] * 2, [[zero] * FIELDS] * 2, state(0), state(LEV - 1))
    half = LEV // 2
    excess, moved, above, below = lax.fori_loop(0, half - 1, eliminate, start, unroll=3)
    weight = interface_weight(eddy, above, below)
    solved = [[], []]
    for f in range(FIELDS):
        m = 0 if f in HEAT else 1
        w = weight[m]
        a = 1.0 + excess[0][m]
        b = 1.0 + excess[1][m]
        inv = 1.0 / (a * b + w * (a + b))
        za = level(right, f, half - 1) + moved[0][f]
        zb = level(right, f, half) + moved[1][f]
        ya = ((b + w) * za + w * zb) * inv
        yb = ((a + w) * zb + w * za) * inv
        put_level(right, f, half - 1, ya)
        put_level(right, f, half, yb)
        solved[0].append(ya)
        solved[1].append(yb)

    def substitute(i, carry):
        step = half - 2 - i
        ks = (step, LEV - 1 - step)
        new = [[], []]
        for side in range(2):
            ratio = [factor[side, m, step] for m in range(2)]
            for f in range(FIELDS):
                m = 0 if f in HEAT else 1
                y = level(right, f, ks[side]) + ratio[m] * carry[side][f]
                put_level(right, f, ks[side], y)
                new[side].append(y)
        return new

    lax.fori_loop(0, half - 1, substitute, solved, unroll=3)


def land(copies, put):
    step = PEERS // len(copies)
    for i, group in enumerate(copies):
        for one in group:
            one.wait()
        lax.fori_loop(i * step, (i + 1) * step, put, 0)


def block_kernel(
    departing, edges, x, rows_in, recv, out, left_rows, right_rows,
    tiles, rows, landed, landed_scalars, turned, wind, right, factor, scalars, sems,
):
    parts = 8
    step = PEERS // parts
    (first,) = copy_chunks([(rows_in, rows)], sems, 0)

    def part(i, offset, size, target):
        peers = pl.ds(i * step, step)
        return recv.at[peers, pl.ds(offset, size), :], target.at[peers]

    head = (SCALARS_AT // 8) * 8
    (turn,) = copy_chunks([(recv.at[:, pl.ds(head, 8), :], landed_scalars)], sems, 1)
    arrivals = copy_chunks([part(i, 0, CAP * FIELDS, landed) for i in range(parts)], sems, 2)
    (last,) = copy_chunks([(x, tiles)], sems, 2 + parts)
    turn.wait()
    for i in range(PEERS // 8):
        lines = landed_scalars[pl.ds(i * 8, 8), SCALARS_AT - head, :]
        for c in range(CAP):
            turned[c, pl.ds(i * 8, 8), :] = pltpu.roll(lines, (LEV - 8 * c) % LEV, 1)
    first.wait()

    def put(p, carry):
        for c in range(CAP):
            row = departing[c, p] * ROW
            rows[pl.ds(row, FIELDS), :] = landed[p, pl.ds(c * FIELDS, FIELDS), :]
            rows[pl.ds(row + FIELDS, 1), :] = turned[c, pl.ds(p, 1), :]
        return carry

    land([[one] for one in arrivals], put)
    last.wait()
    transpose_in(
        lambda g, f: tile_block(tiles, g, f), lambda g, f: row_block(rows, g, f), wind, right
    )
    for g in range(8):
        scalars[0, pl.ds(g * GROUP, LEV), :] = row_block(rows, g, FIELDS).T
    solve(
        wind, right, factor,
        [level(scalars, 0, f) for f in range(FIELDS)],
        level(scalars, 0, FIELDS),
    )
    copies = transpose_out(right, tiles, out, sems)

    def edge(k, carry):
        for side, edge_out in ((0, left_rows), (1, right_rows)):
            j = edges[side, k]
            base = (j >> 3) * 48 + (j & 7)
            edge_out[pl.ds(k * FIELDS, FIELDS), :] = tiles[pl.ds(base, FIELDS, stride=8), :]
        return carry

    lax.fori_loop(0, EDGE, edge, 0, unroll=4)
    for one in copies:
        one.wait()


def span_half(tiles, rows, rates, sunlit, eddy, out, wind, right, factor, sems):
    transpose_in(
        lambda g, f: row_block(rows, g, f), lambda g, f: tile_block(tiles, g, f), wind, right
    )
    lit = 0.5 + sunlit[...].astype(jnp.float32)
    forcing = [
        jnp.concatenate([rates[pl.ds(f, 1), pl.ds(g * 128, 128)] for g in range(8)], axis=0) * lit
        for f in range(FIELDS)
    ]
    solve(wind, right, factor, forcing, eddy[...])
    for one in transpose_out(right, tiles, out, sems):
        one.wait()


def span_kernel(
    arriving, plan, info, inc, rates, sunlit, eddy, rows_in, recv, hop, out,
    tiles, rows, landed, landed_hop, wind, right, factor, sems,
):
    parts = 8
    size = PEERS // parts * MESSAGE
    (first,) = copy_chunks([(rows_in, rows)], sems, 0)
    blocks = [pl.ds(i * size, size) for i in range(parts)]
    arrivals = copy_chunks([(recv.at[one], landed.at[one]) for one in blocks], sems, 1)
    relayed, last = copy_chunks([(hop, landed_hop), (inc, tiles)], sems, 1 + parts)
    first.wait()

    def put(p, carry):
        ahead = info[0, p]
        base = p * MESSAGE + ahead * FIELDS
        for c in range(CAP):
            q = jnp.where(ahead + c < SLOTS, arriving[c, p], DUMP)
            rows[pl.ds(q * ROW, FIELDS), :] = landed[pl.ds(base + c * FIELDS, FIELDS), :]
        return carry

    land([[one] for one in arrivals], put)
    relayed.wait()
    me = device_index()

    def put_relayed(i, carry):
        o, u, _, c = planned(plan, i)
        q = arriving[c, wrap(me - o)]
        source = wrap(me - o + u) * HOP
        rows[pl.ds(q * ROW, FIELDS), :] = landed_hop[pl.ds(source, FIELDS), :]
        return carry

    lax.fori_loop(0, plan[PLAN_COUNT], put_relayed, 0)
    last.wait()
    span_half(tiles, rows, rates, sunlit, eddy, out, wind, right, factor, sems)


def resent_span_kernel(
    arriving, inc, rates, sunlit, eddy, rows_in, recv, out,
    tiles, rows, landed, wind, right, factor, sems,
):
    for one in copy_chunks([(rows_in, rows), (recv, landed), (inc, tiles)], sems, 0):
        one.wait()

    def put(p, carry):
        for c in range(CAP):
            q = arriving[c, p]
            rows[pl.ds(q * ROW, FIELDS), :] = landed[pl.ds(p * RESENT + c * FIELDS, FIELDS), :]
        return carry

    lax.fori_loop(0, PEERS, put, 0)
    span_half(tiles, rows, rates, sunlit, eddy, out, wind, right, factor, sems)


def average_kernel(edges, column, own_left, own_right, far_left, far_right, out, buf, sides, sems):
    load = copy_chunks([(column, buf)], sems, 0)
    load += copy_chunks(
        [(one, sides.at[i]) for i, one in enumerate((own_left, own_right, far_left, far_right))],
        sems, 1,
    )
    for one in load:
        one.wait()

    def body(k, carry):
        for side in range(2):
            j = edges[side, k]
            base = (j >> 3) * 48 + (j & 7)
            rows = pl.ds(k * FIELDS, FIELDS)
            buf[pl.ds(base, FIELDS, stride=8), :] = (sides[side, rows, :] + sides[2 + side, rows, :]) * 0.5
        return carry

    lax.fori_loop(0, EDGE, body, 0, unroll=4)
    for one in copy_chunks(chunked(buf, out, 4), sems, 0):
        one.wait()


def shape(*dims, dtype=jnp.float32):
    return jax.ShapeDtypeStruct(dims, dtype)


def spec(space):
    return pl.BlockSpec(memory_space=space)


def cost(flops, mib):
    return pl.CostEstimate(flops=flops, bytes_accessed=mib * 2**20, transcendentals=0)


def call(kernel, operands, outputs, scratch, sem_count, estimate, more=()):
    return pl.pallas_call(
        kernel,
        out_shape=tuple(one for _, one in outputs),
        in_specs=[spec(space) for space, _ in operands],
        out_specs=tuple(spec(space) for space, _ in outputs),
        scratch_shapes=[
            *(pltpu.VMEM(dims, jnp.float32) for dims in scratch),
            *more,
            pltpu.SemaphoreType.DMA((sem_count,)),
        ],
        compiler_params=pltpu.CompilerParams(vmem_limit_bytes=VMEM_LIMIT),
        cost_estimate=estimate,
    )(*(array for _, array in operands))


def exchange(rows, sublanes):
    return lax.all_to_all(
        rows.reshape(PEERS, sublanes, LEV), ("blk", "sub"), split_axis=0, concat_axis=0, tiled=True
    )


def on_device(
    dynamics_profile_values,
    parameterized_increments,
    ground_exchange_rates,
    sunlit_indicator,
    eddy_coefficient_scale,
    departing_profile_indices,
    arriving_parcel_places,
    resident_parcel_place,
    boundary_profile_indices,
):
    smem, vmem, hbm = pltpu.SMEM, pltpu.VMEM, pl.ANY
    departing = (smem, departing_profile_indices[0].T)
    arriving = (smem, arriving_parcel_places[0].T)
    staying = (smem, resident_parcel_place.reshape(-1))
    edges = (smem, boundary_profile_indices[0])
    x = (hbm, to_tiles(dynamics_profile_values))
    inc = (hbm, to_tiles(parameterized_increments))
    physics = (
        (vmem, ground_exchange_rates),
        (vmem, sunlit_indicator.reshape(8, LEV)),
        (vmem, eddy_coefficient_scale.reshape(8, LEV)),
    )
    whole = (COLS * FIELDS, LEV)
    rows = (ROWS_ALLOC, LEV)
    side = (EDGE * FIELDS, LEV)
    transposed = ((3, 8 * GROUP, LEV), (FIELDS, 8 * GROUP, LEV), (2, 2, LEV // 2, 8, LEV))

    integers = pltpu.VMEM((40, PEERS), jnp.int32)

    send, plan, info = call(
        pack_kernel, ((vmem, departing[1]), (vmem, arriving[1]), x, inc, *physics),
        (
            (hbm, shape(SPARE, LEV)),
            (smem, shape(PLAN, dtype=jnp.int32)),
            (vmem, shape(CAP, PEERS, dtype=jnp.int32)),
        ),
        (whole, whole, rows, rows, (PACKED, LEV)), 1, cost(0, 14),
        (
            integers,
            pltpu.SMEM((40, PEERS), jnp.int32),
            pltpu.SMEM((PEERS,), jnp.int32),
            pltpu.SMEM((PEERS,), jnp.int32),
            pltpu.SemaphoreType.DMA((8,)),
        ),
    )
    plan = (smem, plan)
    recv = exchange(send, MESSAGE)
    span_rows, block_rows = call(
        resident_kernel, (staying, x, inc, *physics), ((vmem, shape(*rows)), (vmem, shape(*rows))),
        (whole, whole, rows, rows), 8, cost(0, 14),
    )
    (hop,) = call(
        relay_kernel, (plan, (hbm, recv), (hbm, block_rows)), ((vmem, shape(PEERS * HOP, LEV)),),
        ((PEERS, 16, LEV),), PEERS, cost(0, 2),
    )
    hop = exchange(hop, HOP)
    column, left_rows, right_rows = call(
        block_kernel, (departing, edges, x, (hbm, block_rows), (hbm, recv)),
        ((hbm, shape(*whole)), (vmem, shape(*side)), (vmem, shape(*side))),
        (
            whole, rows, (PEERS, CAP * FIELDS, LEV), (PEERS, 8, LEV), (CAP, PEERS, LEV),
            *transposed, (1, 8 * GROUP, LEV),
        ),
        11, cost(10**9, 20),
    )
    count = lax.axis_size("blk")
    far_left = lax.ppermute(right_rows, "blk", [(i, (i + 1) % count) for i in range(count)])
    far_right = lax.ppermute(left_rows, "blk", [((i + 1) % count, i) for i in range(count)])

    def relayed():
        return call(
            span_kernel,
            (
                arriving, plan, (smem, info), inc, *physics, (hbm, span_rows),
                (hbm, recv.reshape(SPARE, LEV)), (hbm, hop.reshape(PEERS * HOP, LEV)),
            ),
            ((hbm, shape(*whole)),),
            (whole, rows, (LANDED, LEV), (PEERS * HOP, LEV), *transposed), 11, cost(10**9, 20),
        )[0]

    def resent():
        sent = (PEERS * RESENT, LEV)
        (again,) = call(
            resend_kernel, (departing, x), ((hbm, shape(*sent)),), (whole, rows, sent), 1, cost(0, 8)
        )
        again = exchange(again, RESENT).reshape(sent)
        return call(
            resent_span_kernel, (arriving, inc, *physics, (hbm, span_rows), (hbm, again)),
            ((hbm, shape(*whole)),), (whole, rows, sent, *transposed), 8, cost(10**9, 20),
        )[0]

    span_out = lax.cond(plan[1][PLAN_FAILED] > 0, resent, relayed)
    (column,) = call(
        average_kernel,
        (edges, *((hbm, one) for one in (column, left_rows, right_rows, far_left, far_right))),
        ((hbm, shape(*whole)),),
        (whole, (4, *side)), 5, cost(0, 8),
    )
    return from_tiles(span_out), from_tiles(column)


def solution(mesh):
    one = P(("blk", "sub"))
    placed = (one, one, P(None, ("blk", "sub")), one, one, one, one, one, one)
    return jax.shard_map(
        on_device, mesh=mesh, in_specs=placed, out_specs=(one, one), check_vma=False
    )
```

```python
import jax
import jax.numpy as jnp
from jax import lax
from jax.experimental import pallas as pl
from jax.experimental.pallas import tpu as pltpu
from jax.sharding import PartitionSpec as P

FIELDS = 6
LEV = 128
COLS = 1024
PEERS = 128
CAP = 8
EDGE = 128
ROW = 7
DUMP = COLS
ROWS_ALLOC = 7176
SLOTS = 11
RELAYS = 2
FACTS, ROOM, USED = 0, 1, 2
SCALARS_AT = SLOTS * FIELDS
MESSAGE = 72
HOP = 8
RESENT = CAP * FIELDS
SPARE = PEERS * MESSAGE
PACKED = SPARE + 8
LANDED = SPARE + 32
PLAN = 256
PLAN_COUNT = 128
PLAN_FAILED = 129
GROUP = 137
VMEM_LIMIT = 52 * 2**20
HEAT = (0, 1, 4, 5)
RICHARDSON = {0: 0, 2: 1, 3: 2}


def to_tiles(rows):
    return rows.reshape(COLS // 8, 8, FIELDS, LEV).transpose(0, 2, 1, 3).reshape(COLS * FIELDS, LEV)


def from_tiles(tiles):
    return tiles.reshape(COLS // 8, FIELDS, 8, LEV).transpose(0, 2, 1, 3).reshape(COLS, FIELDS * LEV)


def copy_chunks(pairs, sems, first):
    copies = [
        pltpu.make_async_copy(source, target, sems.at[first + i])
        for i, (source, target) in enumerate(pairs)
    ]
    for one in copies:
        one.start()
    return copies


def chunked(source, target, parts):
    size = source.shape[0] // parts
    return [
        (source.at[pl.ds(i * size, size)], target.at[pl.ds(i * size, size)]) for i in range(parts)
    ]


def spread_rows(tiles, rows, first, count):
    def body(t, carry):
        for f in range(FIELDS):
            rows[pl.ds(t * 8 * ROW + f, 8, stride=ROW), :] = tiles[pl.ds(t * 48 + f * 8, 8), :]
        return carry

    lax.fori_loop(first, first + count, body, 0, unroll=4)


def spread_scalars(rates, sunlit, eddy, rows):
    for g in range(8):
        lanes = pl.ds(g * 128, 128)
        one = pl.ds(g, 1)
        forcing = rates[:, lanes] * (0.5 + sunlit[one, :].astype(jnp.float32))
        part = jnp.concatenate([forcing, eddy[one, :], eddy[one, :]], axis=0)
        square = jnp.concatenate([part] * 16, axis=0).T
        for i in range(16):
            rows[pl.ds((g * 128 + i * 8) * ROW + FIELDS, 8, stride=ROW), :] = square[i * 8 : (i + 1) * 8]


def load_rows(x, inc, rates, sunlit, eddy, x_tiles, inc_tiles, x_rows, inc_rows, sems):
    parts = 4
    x_copies = copy_chunks(chunked(x, x_tiles, parts), sems, 0)
    inc_copies = copy_chunks(chunked(inc, inc_tiles, parts), sems, parts)
    spread_scalars(rates, sunlit, eddy, inc_rows)
    count = COLS // 8 // parts
    for copies, tiles, rows in ((x_copies, x_tiles, x_rows), (inc_copies, inc_tiles, inc_rows)):
        for i, one in enumerate(copies):
            one.wait()
            spread_rows(tiles, rows, i * count, count)


def device_index():
    return lax.axis_index("blk") * lax.axis_size("sub") + lax.axis_index("sub")


def wrap(index):
    return index & (PEERS - 1)


def fill_tables(me, departing, arriving, tables, info):
    out_places = departing[...]
    in_places = arriving[...]
    slot = lax.broadcasted_iota(jnp.int32, (CAP, PEERS), 0)
    peer = lax.broadcasted_iota(jnp.int32, (CAP, PEERS), 1)
    leaving = jnp.sum((out_places < COLS).astype(jnp.int32), axis=0, keepdims=True)
    coming = jnp.sum((in_places < COLS).astype(jnp.int32), axis=0, keepdims=True)
    base = peer * MESSAGE
    place = coming + slot
    tables[0:8] = jnp.minimum(out_places, COLS - 1) * ROW
    tables[8:16] = jnp.where(
        (slot < leaving) & (place < SLOTS), base + place * FIELDS, SPARE
    )
    tables[16:24] = jnp.minimum(in_places, COLS - 1) * ROW
    tables[24:32] = jnp.where(slot < coming, base + slot * FIELDS, SPARE)
    info[...] = jnp.where(slot == 0, leaving, coming)
    leaving, coming = (pltpu.roll(one, PEERS - me, 1) for one in (info[0:1], info[1:2]))
    total = leaving + coming
    blocked = wrap(peer) * 2 % PEERS == 0
    excess = jnp.maximum(total - SLOTS, 0)
    room = jnp.minimum(jnp.maximum(SLOTS - total, 0), RELAYS)
    tables[32:40] = jnp.where(
        slot == FACTS,
        leaving | (coming << 4) | (excess << 8),
        jnp.where(slot == ROOM, jnp.where(blocked, 0, room), blocked.astype(jnp.int32)),
    )


def make_plan(table, plan):
    facts, room, used = (table.at[32 + i] for i in (FACTS, ROOM, USED))

    def offset(o, carry):
        fact = facts[o]
        leaving = fact & 15
        coming = (fact >> 4) & 15
        excess = fact >> 8
        middle = o == PEERS // 2

        def column(t, carry):
            last, count, failed = carry

            def search(state):
                tries, u, _ = state
                u = wrap(u + 1)
                return tries + 1, u, (room[u] == 0) | (used[wrap(o - u)] > 0)

            _, u, taken = lax.while_loop(
                lambda state: state[2] & (state[0] < PEERS), search,
                (jnp.int32(0), last, jnp.bool_(True)),
            )
            found = jnp.logical_not(taken)
            slot = leaving - excess + jnp.where(middle, 2 * t, t)
            mirror_slot = jnp.where(middle, slot + 1, coming - excess + t)
            both = jnp.logical_not(middle) | (2 * t + 1 < excess)

            @pl.when(found)
            def _():
                free = room[u]
                r = SLOTS - free
                room[u] = free - 1
                room[PEERS - u] = free - 1
                used[wrap(o - u)] = 1
                used[wrap(u - o)] = 1
                plan[count] = o | (u << 7) | (r << 14) | (slot << 18)
                plan[count + 1] = (PEERS - o) | ((PEERS - u) << 7) | (r << 14) | (mirror_slot << 18)

            count = count + jnp.where(found, jnp.where(both, 2, 1), 0)
            return u, count, failed | taken.astype(jnp.int32)

        rounds = jnp.where(middle, (excess + 1) >> 1, excess)
        return lax.fori_loop(0, rounds, column, carry)

    zero = jnp.int32(0)
    _, count, failed = lax.fori_loop(1, PEERS // 2 + 1, offset, (zero, zero, zero))
    plan[PLAN_COUNT] = count
    plan[PLAN_FAILED] = failed


def planned(plan, i):
    entry = plan[i]
    o = entry & 127
    u = (entry >> 7) & 127
    return o, u, (entry >> 14) & 15, (entry >> 18) & 15


def pack_kernel(
    departing, arriving, x, inc, rates, sunlit, eddy, send, plan, info,
    x_tiles, inc_tiles, x_rows, inc_rows, packed, tables, places, sems, table_sem,
):
    parts = 4
    x_copies = copy_chunks(chunked(x, x_tiles, parts), sems, 0)
    inc_copies = copy_chunks(chunked(inc, inc_tiles, parts), sems, parts)
    me = device_index()
    fill_tables(me, departing, arriving, tables, info)
    move = pltpu.make_async_copy(tables, places, table_sem.at[0])
    move.start()
    spread_scalars(rates, sunlit, eddy, inc_rows)
    move.wait()
    make_plan(places, plan)
    count = COLS // 8 // parts
    for copies, tiles, rows in ((x_copies, x_tiles, x_rows), (inc_copies, inc_tiles, inc_rows)):
        for i, one in enumerate(copies):
            one.wait()
            spread_rows(tiles, rows, i * count, count)

    def relay(i, carry):
        o, u, r, c = planned(plan, i)
        source = places[c, wrap(me + o)]
        target = wrap(me + u) * MESSAGE + r * FIELDS
        packed[pl.ds(target, FIELDS), :] = x_rows[pl.ds(source, FIELDS), :]
        return carry

    lax.fori_loop(0, plan[PLAN_COUNT], relay, 0)
    group = lax.broadcasted_iota(jnp.int32, (1, LEV), 1) >> 3

    def body(p, carry):
        scalars = jnp.zeros((1, LEV), jnp.float32)
        for c in range(CAP):
            packed[pl.ds(places[8 + c, p], FIELDS), :] = x_rows[pl.ds(places[c, p], FIELDS), :]
            row = places[16 + c, p]
            packed[pl.ds(places[24 + c, p], FIELDS), :] = inc_rows[pl.ds(row, FIELDS), :]
            scalars = jnp.where(group == c, inc_rows[pl.ds(row + FIELDS, 1), :], scalars)
        packed[pl.ds(p * MESSAGE + SCALARS_AT, 1), :] = scalars
        return carry

    parts = 8
    step = PEERS // parts
    size = step * MESSAGE
    copies = []
    for i in range(parts):
        lax.fori_loop(i * step, (i + 1) * step, body, 0)
        part = pl.ds(i * size, size)
        copies += copy_chunks([(packed.at[part], send.at[part])], sems, i)
    for one in copies:
        one.wait()


def relay_kernel(plan, recv, prepared, send, landed, sems):
    del prepared
    me = device_index()
    first = (SLOTS - RELAYS) * FIELDS // 8 * 8
    (copy,) = copy_chunks([(recv.at[:, pl.ds(first, MESSAGE - first), :], landed)], sems, 0)
    copy.wait()

    def forward(i, carry):
        o, u, r, _ = planned(plan, i)
        row = landed[wrap(me - u), pl.ds(r * FIELDS - first, FIELDS), :]
        send[pl.ds(wrap(me + o - u) * HOP, FIELDS), :] = row
        return carry

    lax.fori_loop(0, plan[PLAN_COUNT], forward, 0)


def resend_kernel(departing, x, send, x_tiles, x_rows, packed, sems):
    (copy,) = copy_chunks([(x, x_tiles)], sems, 0)
    copy.wait()
    spread_rows(x_tiles, x_rows, 0, COLS // 8)

    def body(p, carry):
        for c in range(CAP):
            j = jnp.minimum(departing[c, p], COLS - 1)
            packed[pl.ds(p * RESENT + c * FIELDS, FIELDS), :] = x_rows[pl.ds(j * ROW, FIELDS), :]
        return carry

    lax.fori_loop(0, PEERS, body, 0)
    (copy,) = copy_chunks([(packed, send)], sems, 0)
    copy.wait()


def resident_kernel(
    staying, x, inc, rates, sunlit, eddy, span_x, block_inc,
    x_tiles, inc_tiles, x_rows, inc_rows, sems,
):
    load_rows(x, inc, rates, sunlit, eddy, x_tiles, inc_tiles, x_rows, inc_rows, sems)

    def body(t, carry):
        for i in range(8):
            j = t * 8 + i
            q = staying[j]
            span_x[pl.ds(q * ROW, FIELDS), :] = x_rows[pl.ds(j * ROW, FIELDS), :]
            source = jnp.minimum(q, COLS - 1)
            block_inc[pl.ds(j * ROW, ROW), :] = inc_rows[pl.ds(source * ROW, ROW), :]
        return carry

    lax.fori_loop(0, COLS // 8, body, 0)


def tile_block(tiles, g, f):
    return jnp.concatenate(
        [tiles[pl.ds((g * 16 + i) * 48 + f * 8, 8), :] for i in range(16)], axis=0
    )


def row_block(rows, g, f):
    return jnp.concatenate(
        [rows[pl.ds((g * 128 + i * 8) * ROW + f, 8, stride=ROW), :] for i in range(16)], axis=0
    )


def transpose_in(load_x, load_inc, wind, right):
    def body(g, carry):
        for f in range(FIELDS):
            x = load_x(g, f)
            if f in RICHARDSON:
                wind[RICHARDSON[f], pl.ds(g * GROUP, LEV), :] = x.T
            right[f, pl.ds(g * GROUP, LEV), :] = (x + load_inc(g, f)).T
        return carry

    lax.fori_loop(0, 8, body, 0)


def transpose_out(right, tiles, out, sems):
    copies = []
    for g, pair in enumerate(chunked(tiles, out, 8)):
        def body(f, carry):
            block = right[f, pl.ds(g * GROUP, LEV), :].T
            for i in range(16):
                tiles[pl.ds((g * 16 + i) * 48 + f * 8, 8), :] = block[i * 8 : (i + 1) * 8]
            return carry

        lax.fori_loop(0, FIELDS, body, 0, unroll=True)
        copies += copy_chunks([pair], sems, g)
    return copies


def level(ref, f, k):
    return ref[f, pl.ds(k, 8, stride=GROUP), :]


def put_level(ref, f, k, value):
    ref[f, pl.ds(k, 8, stride=GROUP), :] = value


def interface_weight(eddy, upper, lower):
    lapse = upper[0] - lower[0]
    u = upper[1] - lower[1]
    v = upper[2] - lower[2]
    shear = u * u + v * v + 0.1
    unstable = lapse < 0.0
    stable_root = shear + 10.0 * lapse
    top = jnp.where(unstable, shear - 8.0 * lapse, shear * shear)
    bottom = jnp.where(unstable, shear - lapse, stable_root * stable_root)
    wind = eddy * (top / bottom)
    return (1.35 * wind, wind)


def solve(wind, right, factor, forcing, eddy):
    for f in range(FIELDS):
        put_level(right, f, LEV - 1, level(right, f, LEV - 1) + forcing[f])

    def state(k):
        return [level(wind, i, k) for i in range(3)]

    zero = jnp.zeros((8, 128), jnp.float32)

    def eliminate(i, carry):
        excess, moved, above, below = carry
        ks = (i, LEV - 1 - i)
        inner = (state(i + 1), state(LEV - 2 - i))
        weights = (
            interface_weight(eddy, above, inner[0]),
            interface_weight(eddy, inner[1], below),
        )
        new_excess = [[], []]
        new_moved = [[], []]
        for side in range(2):
            ratio = []
            inverse = []
            for m in range(2):
                base = 1.0 + excess[side][m]
                inv = 1.0 / (base + weights[side][m])
                out = weights[side][m] * inv
                factor[side, m, i] = out
                ratio.append(out)
                inverse.append(inv)
                new_excess[side].append(base * out)
            for f in range(FIELDS):
                m = 0 if f in HEAT else 1
                z = level(right, f, ks[side]) + moved[side][f]
                put_level(right, f, ks[side], z * inverse[m])
                new_moved[side].append(z * ratio[m])
        return new_excess, new_moved, inner[0], inner[1]

    start = ([[zero] * 2] * 2, [[zero] * FIELDS] * 2, state(0), state(LEV - 1))
    half = LEV // 2
    excess, moved, above, below = lax.fori_loop(0, half - 1, eliminate, start, unroll=3)
    weight = interface_weight(eddy, above, below)
    solved = [[], []]
    for f in range(FIELDS):
        m = 0 if f in HEAT else 1
        w = weight[m]
        a = 1.0 + excess[0][m]
        b = 1.0 + excess[1][m]
        inv = 1.0 / (a * b + w * (a + b))
        za = level(right, f, half - 1) + moved[0][f]
        zb = level(right, f, half) + moved[1][f]
        ya = ((b + w) * za + w * zb) * inv
        yb = ((a + w) * zb + w * za) * inv
        put_level(right, f, half - 1, ya)
        put_level(right, f, half, yb)
        solved[0].append(ya)
        solved[1].append(yb)

    def substitute(i, carry):
        step = half - 2 - i
        ks = (step, LEV - 1 - step)
        new = [[], []]
        for side in range(2):
            ratio = [factor[side, m, step] for m in range(2)]
            for f in range(FIELDS):
                m = 0 if f in HEAT else 1
                y = level(right, f, ks[side]) + ratio[m] * carry[side][f]
                put_level(right, f, ks[side], y)
                new[side].append(y)
        return new

    lax.fori_loop(0, half - 1, substitute, solved, unroll=3)


def land(copies, put):
    step = PEERS // len(copies)
    for i, group in enumerate(copies):
        for one in group:
            one.wait()
        lax.fori_loop(i * step, (i + 1) * step, put, 0)


def block_kernel(
    departing, edges, x, rows_in, recv, out, left_rows, right_rows,
    tiles, rows, landed, landed_scalars, turned, wind, right, factor, scalars, sems,
):
    parts = 8
    step = PEERS // parts
    (first,) = copy_chunks([(rows_in, rows)], sems, 0)

    def part(i, offset, size, target):
        peers = pl.ds(i * step, step)
        return recv.at[peers, pl.ds(offset, size), :], target.at[peers]

    head = (SCALARS_AT // 8) * 8
    (turn,) = copy_chunks([(recv.at[:, pl.ds(head, 8), :], landed_scalars)], sems, 1)
    arrivals = copy_chunks([part(i, 0, CAP * FIELDS, landed) for i in range(parts)], sems, 2)
    (last,) = copy_chunks([(x, tiles)], sems, 2 + parts)
    turn.wait()
    for i in range(PEERS // 8):
        lines = landed_scalars[pl.ds(i * 8, 8), SCALARS_AT - head, :]
        for c in range(CAP):
            turned[c, pl.ds(i * 8, 8), :] = pltpu.roll(lines, (LEV - 8 * c) % LEV, 1)
    first.wait()

    def put(p, carry):
        for c in range(CAP):
            row = departing[c, p] * ROW
            rows[pl.ds(row, FIELDS), :] = landed[p, pl.ds(c * FIELDS, FIELDS), :]
            rows[pl.ds(row + FIELDS, 1), :] = turned[c, pl.ds(p, 1), :]
        return carry

    land([[one] for one in arrivals], put)
    last.wait()
    transpose_in(
        lambda g, f: tile_block(tiles, g, f), lambda g, f: row_block(rows, g, f), wind, right
    )
    for g in range(8):
        scalars[0, pl.ds(g * GROUP, LEV), :] = row_block(rows, g, FIELDS).T
    solve(
        wind, right, factor,
        [level(scalars, 0, f) for f in range(FIELDS)],
        level(scalars, 0, FIELDS),
    )
    copies = transpose_out(right, tiles, out, sems)

    def edge(k, carry):
        for side, edge_out in ((0, left_rows), (1, right_rows)):
            j = edges[side, k]
            base = (j >> 3) * 48 + (j & 7)
            edge_out[pl.ds(k * FIELDS, FIELDS), :] = tiles[pl.ds(base, FIELDS, stride=8), :]
        return carry

    lax.fori_loop(0, EDGE, edge, 0, unroll=4)
    for one in copies:
        one.wait()


def span_half(tiles, rows, rates, sunlit, eddy, out, wind, right, factor, sems):
    transpose_in(
        lambda g, f: row_block(rows, g, f), lambda g, f: tile_block(tiles, g, f), wind, right
    )
    lit = 0.5 + sunlit[...].astype(jnp.float32)
    forcing = [
        jnp.concatenate([rates[pl.ds(f, 1), pl.ds(g * 128, 128)] for g in range(8)], axis=0) * lit
        for f in range(FIELDS)
    ]
    solve(wind, right, factor, forcing, eddy[...])
    for one in transpose_out(right, tiles, out, sems):
        one.wait()


def span_kernel(
    arriving, plan, info, inc, rates, sunlit, eddy, rows_in, recv, hop, out,
    tiles, rows, landed, landed_hop, wind, right, factor, sems,
):
    parts = 8
    size = PEERS // parts * MESSAGE
    (first,) = copy_chunks([(rows_in, rows)], sems, 0)
    blocks = [pl.ds(i * size, size) for i in range(parts)]
    arrivals = copy_chunks([(recv.at[one], landed.at[one]) for one in blocks], sems, 1)
    relayed, last = copy_chunks([(hop, landed_hop), (inc, tiles)], sems, 1 + parts)
    first.wait()

    def put(p, carry):
        ahead = info[0, p]
        base = p * MESSAGE + ahead * FIELDS
        for c in range(CAP):
            q = jnp.where(ahead + c < SLOTS, arriving[c, p], DUMP)
            rows[pl.ds(q * ROW, FIELDS), :] = landed[pl.ds(base + c * FIELDS, FIELDS), :]
        return carry

    land([[one] for one in arrivals], put)
    relayed.wait()
    me = device_index()

    def put_relayed(i, carry):
        o, u, _, c = planned(plan, i)
        q = arriving[c, wrap(me - o)]
        source = wrap(me - o + u) * HOP
        rows[pl.ds(q * ROW, FIELDS), :] = landed_hop[pl.ds(source, FIELDS), :]
        return carry

    lax.fori_loop(0, plan[PLAN_COUNT], put_relayed, 0)
    last.wait()
    span_half(tiles, rows, rates, sunlit, eddy, out, wind, right, factor, sems)


def resent_span_kernel(
    arriving, inc, rates, sunlit, eddy, rows_in, recv, out,
    tiles, rows, landed, wind, right, factor, sems,
):
    for one in copy_chunks([(rows_in, rows), (recv, landed), (inc, tiles)], sems, 0):
        one.wait()

    def put(p, carry):
        for c in range(CAP):
            q = arriving[c, p]
            rows[pl.ds(q * ROW, FIELDS), :] = landed[pl.ds(p * RESENT + c * FIELDS, FIELDS), :]
        return carry

    lax.fori_loop(0, PEERS, put, 0)
    span_half(tiles, rows, rates, sunlit, eddy, out, wind, right, factor, sems)


def average_kernel(
    edges, column, own_left, own_right, far_left, far_right, after, out, buf, sides, sems
):
    del after
    load = copy_chunks(
        [(one, sides.at[i]) for i, one in enumerate((own_left, far_left, own_right, far_right))],
        sems, 1,
    )
    load += copy_chunks([(column, buf)], sems, 0)
    for one in load[:4]:
        one.wait()
    for side in range(2):
        sides[2 * side] = (sides[2 * side] + sides[2 * side + 1]) * 0.5
    load[4].wait()

    def body(k, carry):
        for side in range(2):
            j = edges[side, k]
            base = (j >> 3) * 48 + (j & 7)
            buf[pl.ds(base, FIELDS, stride=8), :] = sides[2 * side, pl.ds(k * FIELDS, FIELDS), :]
        return carry

    lax.fori_loop(0, EDGE, body, 0, unroll=8)
    for one in copy_chunks(chunked(buf, out, 4), sems, 0):
        one.wait()


def shape(*dims, dtype=jnp.float32):
    return jax.ShapeDtypeStruct(dims, dtype)


def spec(space):
    return pl.BlockSpec(memory_space=space)


def cost(flops, mib):
    return pl.CostEstimate(flops=flops, bytes_accessed=mib * 2**20, transcendentals=0)


def call(kernel, operands, outputs, scratch, sem_count, estimate, more=()):
    return pl.pallas_call(
        kernel,
        out_shape=tuple(one for _, one in outputs),
        in_specs=[spec(space) for space, _ in operands],
        out_specs=tuple(spec(space) for space, _ in outputs),
        scratch_shapes=[
            *(pltpu.VMEM(dims, jnp.float32) for dims in scratch),
            *more,
            pltpu.SemaphoreType.DMA((sem_count,)),
        ],
        compiler_params=pltpu.CompilerParams(vmem_limit_bytes=VMEM_LIMIT),
        cost_estimate=estimate,
    )(*(array for _, array in operands))


def exchange(rows, sublanes):
    return lax.all_to_all(
        rows.reshape(PEERS, sublanes, LEV), ("blk", "sub"), split_axis=0, concat_axis=0, tiled=True
    )


def on_device(
    dynamics_profile_values,
    parameterized_increments,
    ground_exchange_rates,
    sunlit_indicator,
    eddy_coefficient_scale,
    departing_profile_indices,
    arriving_parcel_places,
    resident_parcel_place,
    boundary_profile_indices,
):
    smem, vmem, hbm = pltpu.SMEM, pltpu.VMEM, pl.ANY
    departing = (smem, departing_profile_indices[0].T)
    arriving = (smem, arriving_parcel_places[0].T)
    staying = (smem, resident_parcel_place.reshape(-1))
    edges = (smem, boundary_profile_indices[0])
    x = (hbm, to_tiles(dynamics_profile_values))
    inc = (hbm, to_tiles(parameterized_increments))
    physics = (
        (vmem, ground_exchange_rates),
        (vmem, sunlit_indicator.reshape(8, LEV)),
        (vmem, eddy_coefficient_scale.reshape(8, LEV)),
    )
    whole = (COLS * FIELDS, LEV)
    rows = (ROWS_ALLOC, LEV)
    side = (EDGE * FIELDS, LEV)
    transposed = ((3, 8 * GROUP, LEV), (FIELDS, 8 * GROUP, LEV), (2, 2, LEV // 2, 8, LEV))

    integers = pltpu.VMEM((40, PEERS), jnp.int32)

    send, plan, info = call(
        pack_kernel, ((vmem, departing[1]), (vmem, arriving[1]), x, inc, *physics),
        (
            (hbm, shape(SPARE, LEV)),
            (smem, shape(PLAN, dtype=jnp.int32)),
            (vmem, shape(CAP, PEERS, dtype=jnp.int32)),
        ),
        (whole, whole, rows, rows, (PACKED, LEV)), 1, cost(0, 14),
        (
            integers,
            pltpu.SMEM((40, PEERS), jnp.int32),
            pltpu.SemaphoreType.DMA((8,)),
        ),
    )
    plan = (smem, plan)
    recv = exchange(send, MESSAGE)
    span_rows, block_rows = call(
        resident_kernel, (staying, x, inc, *physics), ((vmem, shape(*rows)), (vmem, shape(*rows))),
        (whole, whole, rows, rows), 8, cost(0, 14),
    )
    (hop,) = call(
        relay_kernel, (plan, (hbm, recv), (hbm, block_rows)), ((vmem, shape(PEERS * HOP, LEV)),),
        ((PEERS, MESSAGE - (SLOTS - RELAYS) * FIELDS // 8 * 8, LEV),), 1, cost(0, 2),
    )
    hop = exchange(hop, HOP)
    column, left_rows, right_rows = call(
        block_kernel, (departing, edges, x, (hbm, block_rows), (hbm, recv)),
        ((hbm, shape(*whole)), (vmem, shape(*side)), (vmem, shape(*side))),
        (
            whole, rows, (PEERS, CAP * FIELDS, LEV), (PEERS, 8, LEV), (CAP, PEERS, LEV),
            *transposed, (1, 8 * GROUP, LEV),
        ),
        11, cost(10**9, 20),
    )
    count = lax.axis_size("blk")
    far_left = lax.ppermute(right_rows, "blk", [(i, (i + 1) % count) for i in range(count)])
    far_right = lax.ppermute(left_rows, "blk", [((i + 1) % count, i) for i in range(count)])

    def relayed():
        return call(
            span_kernel,
            (
                arriving, plan, (smem, info), inc, *physics, (hbm, span_rows),
                (hbm, recv.reshape(SPARE, LEV)), (hbm, hop.reshape(PEERS * HOP, LEV)),
            ),
            ((hbm, shape(*whole)),),
            (whole, rows, (LANDED, LEV), (PEERS * HOP, LEV), *transposed), 11, cost(10**9, 20),
        )[0]

    def resent():
        sent = (PEERS * RESENT, LEV)
        (again,) = call(
            resend_kernel, (departing, x), ((hbm, shape(*sent)),), (whole, rows, sent), 1, cost(0, 8)
        )
        again = exchange(again, RESENT).reshape(sent)
        return call(
            resent_span_kernel, (arriving, inc, *physics, (hbm, span_rows), (hbm, again)),
            ((hbm, shape(*whole)),), (whole, rows, sent, *transposed), 8, cost(10**9, 20),
        )[0]

    span_out = lax.cond(plan[1][PLAN_FAILED] > 0, resent, relayed)
    (column,) = call(
        average_kernel,
        (edges, *((hbm, one) for one in (column, left_rows, right_rows, far_left, far_right, span_out))),
        ((hbm, shape(*whole)),),
        (whole, (4, *side)), 5, cost(0, 8),
    )
    return from_tiles(span_out), from_tiles(column)


def solution(mesh):
    one = P(("blk", "sub"))
    placed = (one, one, P(None, ("blk", "sub")), one, one, one, one, one, one)
    return jax.shard_map(
        on_device, mesh=mesh, in_specs=placed, out_specs=(one, one), check_vma=False
    )
```

```python
import jax
import jax.numpy as jnp
from jax import lax
from jax.experimental import pallas as pl
from jax.experimental.pallas import tpu as pltpu
from jax.sharding import PartitionSpec as P

FIELDS = 6
LEV = 128
COLS = 1024
PEERS = 128
CAP = 8
EDGE = 128
ROW = 7
DUMP = COLS
ROWS_ALLOC = 7176
SLOTS = 11
RELAYS = 2
FACTS, ROOM, USED = 0, 1, 2
SCALARS_AT = SLOTS * FIELDS
MESSAGE = 72
HOP = 8
RESENT = CAP * FIELDS
SPARE = PEERS * MESSAGE
PACKED = SPARE + 8
LANDED = SPARE + 32
PLAN = 256
PLAN_COUNT = 128
PLAN_FAILED = 129
GROUP = 137
VMEM_LIMIT = 52 * 2**20
HEAT = (0, 1, 4, 5)
RICHARDSON = {0: 0, 2: 1, 3: 2}


def to_tiles(rows):
    return rows.reshape(COLS // 8, 8, FIELDS, LEV).transpose(0, 2, 1, 3).reshape(COLS * FIELDS, LEV)


def from_tiles(tiles):
    return tiles.reshape(COLS // 8, FIELDS, 8, LEV).transpose(0, 2, 1, 3).reshape(COLS, FIELDS * LEV)


def copy_chunks(pairs, sems, first):
    copies = [
        pltpu.make_async_copy(source, target, sems.at[first + i])
        for i, (source, target) in enumerate(pairs)
    ]
    for one in copies:
        one.start()
    return copies


def chunked(source, target, parts):
    size = source.shape[0] // parts
    return [
        (source.at[pl.ds(i * size, size)], target.at[pl.ds(i * size, size)]) for i in range(parts)
    ]


def spread_rows(tiles, rows, first, count):
    def body(t, carry):
        for f in range(FIELDS):
            rows[pl.ds(t * 8 * ROW + f, 8, stride=ROW), :] = tiles[pl.ds(t * 48 + f * 8, 8), :]
        return carry

    lax.fori_loop(first, first + count, body, 0, unroll=4)


def spread_scalars(rates, sunlit, eddy, rows):
    for g in range(8):
        lanes = pl.ds(g * 128, 128)
        one = pl.ds(g, 1)
        forcing = rates[:, lanes] * (0.5 + sunlit[one, :].astype(jnp.float32))
        part = jnp.concatenate([forcing, eddy[one, :], eddy[one, :]], axis=0)
        square = jnp.concatenate([part] * 16, axis=0).T
        for i in range(16):
            rows[pl.ds((g * 128 + i * 8) * ROW + FIELDS, 8, stride=ROW), :] = square[i * 8 : (i + 1) * 8]


def load_rows(x, inc, rates, sunlit, eddy, x_tiles, inc_tiles, x_rows, inc_rows, sems):
    parts = 4
    x_copies = copy_chunks(chunked(x, x_tiles, parts), sems, 0)
    inc_copies = copy_chunks(chunked(inc, inc_tiles, parts), sems, parts)
    spread_scalars(rates, sunlit, eddy, inc_rows)
    count = COLS // 8 // parts
    for copies, tiles, rows in ((x_copies, x_tiles, x_rows), (inc_copies, inc_tiles, inc_rows)):
        for i, one in enumerate(copies):
            one.wait()
            spread_rows(tiles, rows, i * count, count)


def device_index():
    return lax.axis_index("blk") * lax.axis_size("sub") + lax.axis_index("sub")


def wrap(index):
    return index & (PEERS - 1)


def fill_tables(me, departing, arriving, tables, info):
    out_places = departing[...]
    in_places = arriving[...]
    slot = lax.broadcasted_iota(jnp.int32, (CAP, PEERS), 0)
    peer = lax.broadcasted_iota(jnp.int32, (CAP, PEERS), 1)
    leaving = jnp.sum((out_places < COLS).astype(jnp.int32), axis=0, keepdims=True)
    coming = jnp.sum((in_places < COLS).astype(jnp.int32), axis=0, keepdims=True)
    base = peer * MESSAGE
    place = coming + slot
    tables[0:8] = jnp.minimum(out_places, COLS - 1) * ROW
    tables[8:16] = jnp.where(
        (slot < leaving) & (place < SLOTS), base + place * FIELDS, SPARE
    )
    tables[16:24] = jnp.minimum(in_places, COLS - 1) * ROW
    tables[24:32] = jnp.where(slot < coming, base + slot * FIELDS, SPARE)
    info[...] = jnp.where(slot == 0, leaving, coming)
    leaving, coming = (pltpu.roll(one, PEERS - me, 1) for one in (info[0:1], info[1:2]))
    total = leaving + coming
    blocked = wrap(peer) * 2 % PEERS == 0
    excess = jnp.maximum(total - SLOTS, 0)
    room = jnp.minimum(jnp.maximum(SLOTS - total, 0), RELAYS)
    tables[32:40] = jnp.where(
        slot == FACTS,
        leaving | (coming << 4) | (excess << 8),
        jnp.where(slot == ROOM, jnp.where(blocked, 0, room), blocked.astype(jnp.int32)),
    )


def make_plan(table, plan):
    facts, room, used = (table.at[32 + i] for i in (FACTS, ROOM, USED))

    def offset(o, carry):
        fact = facts[o]
        leaving = fact & 15
        coming = (fact >> 4) & 15
        excess = fact >> 8
        middle = o == PEERS // 2

        def column(t, carry):
            last, count, failed = carry

            def search(state):
                tries, u, _ = state
                u = wrap(u + 1)
                return tries + 1, u, (room[u] == 0) | (used[wrap(o - u)] > 0)

            _, u, taken = lax.while_loop(
                lambda state: state[2] & (state[0] < PEERS), search,
                (jnp.int32(0), last, jnp.bool_(True)),
            )
            found = jnp.logical_not(taken)
            slot = leaving - excess + jnp.where(middle, 2 * t, t)
            mirror_slot = jnp.where(middle, slot + 1, coming - excess + t)
            both = jnp.logical_not(middle) | (2 * t + 1 < excess)

            @pl.when(found)
            def _():
                free = room[u]
                r = SLOTS - free
                room[u] = free - 1
                room[PEERS - u] = free - 1
                used[wrap(o - u)] = 1
                used[wrap(u - o)] = 1
                plan[count] = o | (u << 7) | (r << 14) | (slot << 18)
                plan[count + 1] = (PEERS - o) | ((PEERS - u) << 7) | (r << 14) | (mirror_slot << 18)

            count = count + jnp.where(found, jnp.where(both, 2, 1), 0)
            return u, count, failed | taken.astype(jnp.int32)

        rounds = jnp.where(middle, (excess + 1) >> 1, excess)
        return lax.fori_loop(0, rounds, column, carry)

    zero = jnp.int32(0)
    _, count, failed = lax.fori_loop(1, PEERS // 2 + 1, offset, (zero, zero, zero))
    plan[PLAN_COUNT] = count
    plan[PLAN_FAILED] = failed


def planned(plan, i):
    entry = plan[i]
    o = entry & 127
    u = (entry >> 7) & 127
    return o, u, (entry >> 14) & 15, (entry >> 18) & 15


def pack_kernel(
    departing, arriving, x, inc, rates, sunlit, eddy, send, plan, info,
    x_tiles, inc_tiles, x_rows, inc_rows, packed, tables, places, sems, table_sem,
):
    parts = 4
    x_copies = copy_chunks(chunked(x, x_tiles, parts), sems, 0)
    inc_copies = copy_chunks(chunked(inc, inc_tiles, parts), sems, parts)
    me = device_index()
    fill_tables(me, departing, arriving, tables, info)
    move = pltpu.make_async_copy(tables, places, table_sem.at[0])
    move.start()
    spread_scalars(rates, sunlit, eddy, inc_rows)
    move.wait()
    make_plan(places, plan)
    count = COLS // 8 // parts
    for copies, tiles, rows in ((x_copies, x_tiles, x_rows), (inc_copies, inc_tiles, inc_rows)):
        for i, one in enumerate(copies):
            one.wait()
            spread_rows(tiles, rows, i * count, count)

    def relay(i, carry):
        o, u, r, c = planned(plan, i)
        source = places[c, wrap(me + o)]
        target = wrap(me + u) * MESSAGE + r * FIELDS
        packed[pl.ds(target, FIELDS), :] = x_rows[pl.ds(source, FIELDS), :]
        return carry

    lax.fori_loop(0, plan[PLAN_COUNT], relay, 0)
    group = lax.broadcasted_iota(jnp.int32, (1, LEV), 1) >> 3

    def body(p, carry):
        scalars = jnp.zeros((1, LEV), jnp.float32)
        for c in range(CAP):
            packed[pl.ds(places[8 + c, p], FIELDS), :] = x_rows[pl.ds(places[c, p], FIELDS), :]
            row = places[16 + c, p]
            packed[pl.ds(places[24 + c, p], FIELDS), :] = inc_rows[pl.ds(row, FIELDS), :]
            scalars = jnp.where(group == c, inc_rows[pl.ds(row + FIELDS, 1), :], scalars)
        packed[pl.ds(p * MESSAGE + SCALARS_AT, 1), :] = scalars
        return carry

    parts = 8
    step = PEERS // parts
    size = step * MESSAGE
    copies = []
    for i in range(parts):
        lax.fori_loop(i * step, (i + 1) * step, body, 0)
        part = pl.ds(i * size, size)
        copies += copy_chunks([(packed.at[part], send.at[part])], sems, i)
    for one in copies:
        one.wait()


def relay_kernel(plan, recv, prepared, send, landed, sems):
    del prepared
    me = device_index()
    first = (SLOTS - RELAYS) * FIELDS // 8 * 8
    (copy,) = copy_chunks([(recv.at[:, pl.ds(first, MESSAGE - first), :], landed)], sems, 0)
    copy.wait()

    def forward(i, carry):
        o, u, r, _ = planned(plan, i)
        row = landed[wrap(me - u), pl.ds(r * FIELDS - first, FIELDS), :]
        send[pl.ds(wrap(me + o - u) * HOP, FIELDS), :] = row
        return carry

    lax.fori_loop(0, plan[PLAN_COUNT], forward, 0)


def resend_kernel(departing, x, send, x_tiles, x_rows, packed, sems):
    (copy,) = copy_chunks([(x, x_tiles)], sems, 0)
    copy.wait()
    spread_rows(x_tiles, x_rows, 0, COLS // 8)

    def body(p, carry):
        for c in range(CAP):
            j = jnp.minimum(departing[c, p], COLS - 1)
            packed[pl.ds(p * RESENT + c * FIELDS, FIELDS), :] = x_rows[pl.ds(j * ROW, FIELDS), :]
        return carry

    lax.fori_loop(0, PEERS, body, 0)
    (copy,) = copy_chunks([(packed, send)], sems, 0)
    copy.wait()


def resident_kernel(
    staying, x, inc, rates, sunlit, eddy, span_x, block_inc, x_turned, inc_turned, stable,
    x_tiles, inc_tiles, x_rows, inc_rows, sems,
):
    load_rows(x, inc, rates, sunlit, eddy, x_tiles, inc_tiles, x_rows, inc_rows, sems)

    def body(t, carry):
        for i in range(8):
            j = t * 8 + i
            q = staying[j]
            span_x[pl.ds(q * ROW, FIELDS), :] = x_rows[pl.ds(j * ROW, FIELDS), :]
            source = jnp.minimum(q, COLS - 1)
            block_inc[pl.ds(j * ROW, ROW), :] = inc_rows[pl.ds(source * ROW, ROW), :]
        return carry

    lax.fori_loop(0, COLS // 8, body, 0)
    turn(lambda g, f: tile_block(x_tiles, g, f), x_turned)
    turn(lambda g, f: tile_block(inc_tiles, g, f), inc_turned)

    def state(k):
        return [level(x_turned, f, k) for f in RICHARDSON]

    def interface(k, above):
        below = state(k + 1)
        stable[k] = stability_between(above, below)
        return below

    lax.fori_loop(0, LEV - 1, interface, state(0), unroll=2)
    stable[LEV - 1] = jnp.zeros((8, LEV), jnp.float32)


def tile_block(tiles, g, f):
    return jnp.concatenate(
        [tiles[pl.ds((g * 16 + i) * 48 + f * 8, 8), :] for i in range(16)], axis=0
    )


def row_block(rows, g, f):
    return jnp.concatenate(
        [rows[pl.ds((g * 128 + i * 8) * ROW + f, 8, stride=ROW), :] for i in range(16)], axis=0
    )


def turn(load, turned):
    def body(g, carry):
        for f in range(FIELDS):
            turned[f, pl.ds(g * GROUP, LEV), :] = load(g, f).T
        return carry

    lax.fori_loop(0, 8, body, 0)


def turn_onto(load, right, wind=None):
    def body(g, carry):
        for f in range(FIELDS):
            lines = pl.ds(g * GROUP, LEV)
            block = load(g, f).T
            if wind is not None and f in RICHARDSON:
                wind[RICHARDSON[f], lines, :] = block
            right[f, lines, :] = right[f, lines, :] + block
        return carry

    lax.fori_loop(0, 8, body, 0)


def transpose_out(right, tiles, out, sems):
    copies = []
    for g, pair in enumerate(chunked(tiles, out, 8)):
        def body(f, carry):
            block = right[f, pl.ds(g * GROUP, LEV), :].T
            for i in range(16):
                tiles[pl.ds((g * 16 + i) * 48 + f * 8, 8), :] = block[i * 8 : (i + 1) * 8]
            return carry

        lax.fori_loop(0, FIELDS, body, 0, unroll=True)
        copies += copy_chunks([pair], sems, g)
    return copies


def level(ref, f, k):
    return ref[f, pl.ds(k, 8, stride=GROUP), :]


def put_level(ref, f, k, value):
    ref[f, pl.ds(k, 8, stride=GROUP), :] = value


def stability_between(upper, lower):
    lapse = upper[0] - lower[0]
    u = upper[1] - lower[1]
    v = upper[2] - lower[2]
    shear = u * u + v * v + 0.1
    unstable = lapse < 0.0
    stable_root = shear + 10.0 * lapse
    top = jnp.where(unstable, shear - 8.0 * lapse, shear * shear)
    bottom = jnp.where(unstable, shear - lapse, stable_root * stable_root)
    return top / bottom


def weight_pair(eddy, stability):
    wind = eddy * stability
    return (1.35 * wind, wind)


def wind_state(wind):
    return lambda k: [level(wind, i, k) for i in range(3)]


def solve(right, factor, forcing, eddy, state, stability):
    for f in range(FIELDS):
        put_level(right, f, LEV - 1, level(right, f, LEV - 1) + forcing[f])

    zero = jnp.zeros((8, 128), jnp.float32)

    def eliminate(i, carry):
        excess, moved, above, below = carry
        ks = (i, LEV - 1 - i)
        inner = (state(i + 1), state(LEV - 2 - i))
        weights = (
            weight_pair(eddy, stability(above, inner[0], i)),
            weight_pair(eddy, stability(inner[1], below, LEV - 2 - i)),
        )
        new_excess = [[], []]
        new_moved = [[], []]
        for side in range(2):
            ratio = []
            inverse = []
            for m in range(2):
                base = 1.0 + excess[side][m]
                inv = 1.0 / (base + weights[side][m])
                out = weights[side][m] * inv
                factor[side, m, i] = out
                ratio.append(out)
                inverse.append(inv)
                new_excess[side].append(base * out)
            for f in range(FIELDS):
                m = 0 if f in HEAT else 1
                z = level(right, f, ks[side]) + moved[side][f]
                put_level(right, f, ks[side], z * inverse[m])
                new_moved[side].append(z * ratio[m])
        return new_excess, new_moved, inner[0], inner[1]

    start = ([[zero] * 2] * 2, [[zero] * FIELDS] * 2, state(0), state(LEV - 1))
    half = LEV // 2
    excess, moved, above, below = lax.fori_loop(0, half - 1, eliminate, start, unroll=3)
    weight = weight_pair(eddy, stability(above, below, half - 1))
    solved = [[], []]
    for f in range(FIELDS):
        m = 0 if f in HEAT else 1
        w = weight[m]
        a = 1.0 + excess[0][m]
        b = 1.0 + excess[1][m]
        inv = 1.0 / (a * b + w * (a + b))
        za = level(right, f, half - 1) + moved[0][f]
        zb = level(right, f, half) + moved[1][f]
        ya = ((b + w) * za + w * zb) * inv
        yb = ((a + w) * zb + w * za) * inv
        put_level(right, f, half - 1, ya)
        put_level(right, f, half, yb)
        solved[0].append(ya)
        solved[1].append(yb)

    def substitute(i, carry):
        step = half - 2 - i
        ks = (step, LEV - 1 - step)
        new = [[], []]
        for side in range(2):
            ratio = [factor[side, m, step] for m in range(2)]
            for f in range(FIELDS):
                m = 0 if f in HEAT else 1
                y = level(right, f, ks[side]) + ratio[m] * carry[side][f]
                put_level(right, f, ks[side], y)
                new[side].append(y)
        return new

    lax.fori_loop(0, half - 1, substitute, solved, unroll=3)


def land(copies, put):
    step = PEERS // len(copies)
    for i, group in enumerate(copies):
        for one in group:
            one.wait()
        lax.fori_loop(i * step, (i + 1) * step, put, 0)


def block_kernel(
    departing, edges, x_turned, stable_in, rows_in, recv, out, left_rows, right_rows,
    tiles, rows, landed, landed_scalars, turned, stable, right, factor, scalars, sems,
):
    parts = 8
    step = PEERS // parts
    (first,) = copy_chunks([(rows_in, rows)], sems, 0)

    def part(i, offset, size, target):
        peers = pl.ds(i * step, step)
        return recv.at[peers, pl.ds(offset, size), :], target.at[peers]

    head = (SCALARS_AT // 8) * 8
    (turn,) = copy_chunks([(recv.at[:, pl.ds(head, 8), :], landed_scalars)], sems, 1)
    arrivals = copy_chunks([part(i, 0, CAP * FIELDS, landed) for i in range(parts)], sems, 2)
    last = copy_chunks([(x_turned, right), (stable_in, stable)], sems, 2 + parts)
    turn.wait()
    for i in range(PEERS // 8):
        lines = landed_scalars[pl.ds(i * 8, 8), SCALARS_AT - head, :]
        for c in range(CAP):
            turned[c, pl.ds(i * 8, 8), :] = pltpu.roll(lines, (LEV - 8 * c) % LEV, 1)
    first.wait()

    def put(p, carry):
        for c in range(CAP):
            row = departing[c, p] * ROW
            rows[pl.ds(row, FIELDS), :] = landed[p, pl.ds(c * FIELDS, FIELDS), :]
            rows[pl.ds(row + FIELDS, 1), :] = turned[c, pl.ds(p, 1), :]
        return carry

    land([[one] for one in arrivals], put)
    for one in last:
        one.wait()
    turn_onto(lambda g, f: row_block(rows, g, f), right)
    for g in range(8):
        scalars[0, pl.ds(g * GROUP, LEV), :] = row_block(rows, g, FIELDS).T
    solve(
        right, factor,
        [level(scalars, 0, f) for f in range(FIELDS)],
        level(scalars, 0, FIELDS),
        lambda k: [],
        lambda upper, lower, k: stable[k],
    )
    copies = transpose_out(right, tiles, out, sems)

    def edge(k, carry):
        for side, edge_out in ((0, left_rows), (1, right_rows)):
            j = edges[side, k]
            base = (j >> 3) * 48 + (j & 7)
            edge_out[pl.ds(k * FIELDS, FIELDS), :] = tiles[pl.ds(base, FIELDS, stride=8), :]
        return carry

    lax.fori_loop(0, EDGE, edge, 0, unroll=4)
    for one in copies:
        one.wait()


def span_half(tiles, rows, rates, sunlit, eddy, out, wind, right, factor, sems):
    turn_onto(lambda g, f: row_block(rows, g, f), right, wind)
    lit = 0.5 + sunlit[...].astype(jnp.float32)
    forcing = [
        jnp.concatenate([rates[pl.ds(f, 1), pl.ds(g * 128, 128)] for g in range(8)], axis=0) * lit
        for f in range(FIELDS)
    ]
    solve(
        right, factor, forcing, eddy[...], wind_state(wind),
        lambda upper, lower, k: stability_between(upper, lower),
    )
    for one in transpose_out(right, tiles, out, sems):
        one.wait()


def span_kernel(
    arriving, plan, info, inc_turned, rates, sunlit, eddy, rows_in, recv, hop, out,
    tiles, rows, landed, landed_hop, wind, right, factor, sems,
):
    parts = 8
    size = PEERS // parts * MESSAGE
    (first,) = copy_chunks([(rows_in, rows)], sems, 0)
    blocks = [pl.ds(i * size, size) for i in range(parts)]
    arrivals = copy_chunks([(recv.at[one], landed.at[one]) for one in blocks], sems, 1)
    relayed, last = copy_chunks([(hop, landed_hop), (inc_turned, right)], sems, 1 + parts)
    first.wait()

    def put(p, carry):
        ahead = info[0, p]
        base = p * MESSAGE + ahead * FIELDS
        for c in range(CAP):
            q = jnp.where(ahead + c < SLOTS, arriving[c, p], DUMP)
            rows[pl.ds(q * ROW, FIELDS), :] = landed[pl.ds(base + c * FIELDS, FIELDS), :]
        return carry

    land([[one] for one in arrivals], put)
    relayed.wait()
    me = device_index()

    def put_relayed(i, carry):
        o, u, _, c = planned(plan, i)
        q = arriving[c, wrap(me - o)]
        source = wrap(me - o + u) * HOP
        rows[pl.ds(q * ROW, FIELDS), :] = landed_hop[pl.ds(source, FIELDS), :]
        return carry

    lax.fori_loop(0, plan[PLAN_COUNT], put_relayed, 0)
    last.wait()
    span_half(tiles, rows, rates, sunlit, eddy, out, wind, right, factor, sems)


def resent_span_kernel(
    arriving, inc_turned, rates, sunlit, eddy, rows_in, recv, out,
    tiles, rows, landed, wind, right, factor, sems,
):
    for one in copy_chunks([(rows_in, rows), (recv, landed), (inc_turned, right)], sems, 0):
        one.wait()

    def put(p, carry):
        for c in range(CAP):
            q = arriving[c, p]
            rows[pl.ds(q * ROW, FIELDS), :] = landed[pl.ds(p * RESENT + c * FIELDS, FIELDS), :]
        return carry

    lax.fori_loop(0, PEERS, put, 0)
    span_half(tiles, rows, rates, sunlit, eddy, out, wind, right, factor, sems)


def average_kernel(
    edges, column, own_left, own_right, far_left, far_right, after, out, buf, sides, sems
):
    del after
    load = copy_chunks(
        [(one, sides.at[i]) for i, one in enumerate((own_left, far_left, own_right, far_right))],
        sems, 1,
    )
    load += copy_chunks([(column, buf)], sems, 0)
    for one in load[:4]:
        one.wait()
    for side in range(2):
        sides[2 * side] = (sides[2 * side] + sides[2 * side + 1]) * 0.5
    load[4].wait()

    def body(k, carry):
        for side in range(2):
            j = edges[side, k]
            base = (j >> 3) * 48 + (j & 7)
            buf[pl.ds(base, FIELDS, stride=8), :] = sides[2 * side, pl.ds(k * FIELDS, FIELDS), :]
        return carry

    lax.fori_loop(0, EDGE, body, 0, unroll=8)
    for one in copy_chunks(chunked(buf, out, 4), sems, 0):
        one.wait()


def shape(*dims, dtype=jnp.float32):
    return jax.ShapeDtypeStruct(dims, dtype)


def spec(space):
    return pl.BlockSpec(memory_space=space)


def cost(flops, mib):
    return pl.CostEstimate(flops=flops, bytes_accessed=mib * 2**20, transcendentals=0)


def call(kernel, operands, outputs, scratch, sem_count, estimate, more=()):
    return pl.pallas_call(
        kernel,
        out_shape=tuple(one for _, one in outputs),
        in_specs=[spec(space) for space, _ in operands],
        out_specs=tuple(spec(space) for space, _ in outputs),
        scratch_shapes=[
            *(pltpu.VMEM(dims, jnp.float32) for dims in scratch),
            *more,
            pltpu.SemaphoreType.DMA((sem_count,)),
        ],
        compiler_params=pltpu.CompilerParams(vmem_limit_bytes=VMEM_LIMIT),
        cost_estimate=estimate,
    )(*(array for _, array in operands))


def exchange(rows, sublanes):
    return lax.all_to_all(
        rows.reshape(PEERS, sublanes, LEV), ("blk", "sub"), split_axis=0, concat_axis=0, tiled=True
    )


def on_device(
    dynamics_profile_values,
    parameterized_increments,
    ground_exchange_rates,
    sunlit_indicator,
    eddy_coefficient_scale,
    departing_profile_indices,
    arriving_parcel_places,
    resident_parcel_place,
    boundary_profile_indices,
):
    smem, vmem, hbm = pltpu.SMEM, pltpu.VMEM, pl.ANY
    departing = (smem, departing_profile_indices[0].T)
    arriving = (smem, arriving_parcel_places[0].T)
    staying = (smem, resident_parcel_place.reshape(-1))
    edges = (smem, boundary_profile_indices[0])
    x = (hbm, to_tiles(dynamics_profile_values))
    inc = (hbm, to_tiles(parameterized_increments))
    physics = (
        (vmem, ground_exchange_rates),
        (vmem, sunlit_indicator.reshape(8, LEV)),
        (vmem, eddy_coefficient_scale.reshape(8, LEV)),
    )
    whole = (COLS * FIELDS, LEV)
    rows = (ROWS_ALLOC, LEV)
    side = (EDGE * FIELDS, LEV)
    stable_dims = (LEV, 8, LEV)
    transposed = ((3, 8 * GROUP, LEV), (FIELDS, 8 * GROUP, LEV), (2, 2, LEV // 2, 8, LEV))

    integers = pltpu.VMEM((40, PEERS), jnp.int32)

    send, plan, info = call(
        pack_kernel, ((vmem, departing[1]), (vmem, arriving[1]), x, inc, *physics),
        (
            (hbm, shape(SPARE, LEV)),
            (smem, shape(PLAN, dtype=jnp.int32)),
            (vmem, shape(CAP, PEERS, dtype=jnp.int32)),
        ),
        (whole, whole, rows, rows, (PACKED, LEV)), 1, cost(0, 14),
        (
            integers,
            pltpu.SMEM((40, PEERS), jnp.int32),
            pltpu.SemaphoreType.DMA((8,)),
        ),
    )
    plan = (smem, plan)
    recv = exchange(send, MESSAGE)
    span_rows, block_rows, x_turned, inc_turned, stable = call(
        resident_kernel, (staying, x, inc, *physics),
        tuple((vmem, shape(*dims)) for dims in (rows, rows, transposed[1], transposed[1], stable_dims)),
        (whole, whole, rows, rows), 8, cost(0, 14),
    )
    failed, block_rows = lax.optimization_barrier((plan[1][PLAN_FAILED], block_rows))
    (hop,) = call(
        relay_kernel, (plan, (hbm, recv), (hbm, block_rows)), ((vmem, shape(PEERS * HOP, LEV)),),
        ((PEERS, MESSAGE - (SLOTS - RELAYS) * FIELDS // 8 * 8, LEV),), 1, cost(0, 2),
    )
    hop = exchange(hop, HOP)
    column, left_rows, right_rows = call(
        block_kernel,
        (departing, edges, *((hbm, one) for one in (x_turned, stable, block_rows, recv))),
        ((hbm, shape(*whole)), (vmem, shape(*side)), (vmem, shape(*side))),
        (
            whole, rows, (PEERS, CAP * FIELDS, LEV), (PEERS, 8, LEV), (CAP, PEERS, LEV),
            stable_dims, *transposed[1:], (1, 8 * GROUP, LEV),
        ),
        12, cost(10**9, 20),
    )
    count = lax.axis_size("blk")
    far_left = lax.ppermute(right_rows, "blk", [(i, (i + 1) % count) for i in range(count)])
    far_right = lax.ppermute(left_rows, "blk", [((i + 1) % count, i) for i in range(count)])

    def relayed():
        return call(
            span_kernel,
            (
                arriving, plan, (smem, info), (hbm, inc_turned), *physics, (hbm, span_rows),
                (hbm, recv.reshape(SPARE, LEV)), (hbm, hop.reshape(PEERS * HOP, LEV)),
            ),
            ((hbm, shape(*whole)),),
            (whole, rows, (LANDED, LEV), (PEERS * HOP, LEV), *transposed), 11, cost(10**9, 20),
        )[0]

    def resent():
        sent = (PEERS * RESENT, LEV)
        (again,) = call(
            resend_kernel, (departing, x), ((hbm, shape(*sent)),), (whole, rows, sent), 1, cost(0, 8)
        )
        again = exchange(again, RESENT).reshape(sent)
        return call(
            resent_span_kernel,
            (arriving, (hbm, inc_turned), *physics, (hbm, span_rows), (hbm, again)),
            ((hbm, shape(*whole)),), (whole, rows, sent, *transposed), 8, cost(10**9, 20),
        )[0]

    span_out = lax.cond(failed > 0, resent, relayed)
    (column,) = call(
        average_kernel,
        (edges, *((hbm, one) for one in (column, left_rows, right_rows, far_left, far_right, span_out))),
        ((hbm, shape(*whole)),),
        (whole, (4, *side)), 5, cost(0, 8),
    )
    return from_tiles(span_out), from_tiles(column)


def solution(mesh):
    one = P(("blk", "sub"))
    placed = (one, one, P(None, ("blk", "sub")), one, one, one, one, one, one)
    return jax.shard_map(
        on_device, mesh=mesh, in_specs=placed, out_specs=(one, one), check_vma=False
    )
```

```python
import jax
import jax.numpy as jnp
from jax import lax
from jax.experimental import pallas as pl
from jax.experimental.pallas import tpu as pltpu
from jax.sharding import PartitionSpec as P

FIELDS = 6
LEV = 128
COLS = 1024
PEERS = 128
CAP = 8
EDGE = 128
ROW = 7
DUMP = COLS
ROWS_ALLOC = 7176
SLOTS = 11
RELAYS = 2
FACTS, ROOM, USED = 0, 1, 2
SCALARS_AT = SLOTS * FIELDS
MESSAGE = 72
HOP = 8
RESENT = CAP * FIELDS
SPARE = PEERS * MESSAGE
PACKED = SPARE + 8
LANDED = SPARE + 32
PLAN = 256
PLAN_COUNT = 128
PLAN_FAILED = 129
GROUP = 137
VMEM_LIMIT = 52 * 2**20
HEAT = (0, 1, 4, 5)
RICHARDSON = {0: 0, 2: 1, 3: 2}


def to_tiles(rows):
    return rows.reshape(COLS // 8, 8, FIELDS, LEV).transpose(0, 2, 1, 3).reshape(COLS * FIELDS, LEV)


def from_tiles(tiles):
    return tiles.reshape(COLS // 8, FIELDS, 8, LEV).transpose(0, 2, 1, 3).reshape(COLS, FIELDS * LEV)


def copy_chunks(pairs, sems, first):
    copies = [
        pltpu.make_async_copy(source, target, sems.at[first + i])
        for i, (source, target) in enumerate(pairs)
    ]
    for one in copies:
        one.start()
    return copies


def chunked(source, target, parts):
    size = source.shape[0] // parts
    return [
        (source.at[pl.ds(i * size, size)], target.at[pl.ds(i * size, size)]) for i in range(parts)
    ]


def spread_rows(tiles, rows, first, count):
    def body(t, carry):
        for f in range(FIELDS):
            rows[pl.ds(t * 8 * ROW + f, 8, stride=ROW), :] = tiles[pl.ds(t * 48 + f * 8, 8), :]
        return carry

    lax.fori_loop(first, first + count, body, 0, unroll=4)


def spread_scalars(rates, sunlit, eddy, rows):
    for g in range(8):
        lanes = pl.ds(g * 128, 128)
        one = pl.ds(g, 1)
        forcing = rates[:, lanes] * (0.5 + sunlit[one, :].astype(jnp.float32))
        part = jnp.concatenate([forcing, eddy[one, :], eddy[one, :]], axis=0)
        square = jnp.concatenate([part] * 16, axis=0).T
        for i in range(16):
            rows[pl.ds((g * 128 + i * 8) * ROW + FIELDS, 8, stride=ROW), :] = square[i * 8 : (i + 1) * 8]


def load_rows(x, inc, rates, sunlit, eddy, x_tiles, inc_tiles, x_rows, inc_rows, sems):
    parts = 4
    x_copies = copy_chunks(chunked(x, x_tiles, parts), sems, 0)
    inc_copies = copy_chunks(chunked(inc, inc_tiles, parts), sems, parts)
    spread_scalars(rates, sunlit, eddy, inc_rows)
    count = COLS // 8 // parts
    for copies, tiles, rows in ((x_copies, x_tiles, x_rows), (inc_copies, inc_tiles, inc_rows)):
        for i, one in enumerate(copies):
            one.wait()
            spread_rows(tiles, rows, i * count, count)


def device_index():
    return lax.axis_index("blk") * lax.axis_size("sub") + lax.axis_index("sub")


def wrap(index):
    return index & (PEERS - 1)


def fill_tables(me, departing, arriving, tables, info):
    out_places = departing[...]
    in_places = arriving[...]
    slot = lax.broadcasted_iota(jnp.int32, (CAP, PEERS), 0)
    peer = lax.broadcasted_iota(jnp.int32, (CAP, PEERS), 1)
    leaving = jnp.sum((out_places < COLS).astype(jnp.int32), axis=0, keepdims=True)
    coming = jnp.sum((in_places < COLS).astype(jnp.int32), axis=0, keepdims=True)
    base = peer * MESSAGE
    place = coming + slot
    tables[0:8] = jnp.minimum(out_places, COLS - 1) * ROW
    tables[8:16] = jnp.where(
        (slot < leaving) & (place < SLOTS), base + place * FIELDS, SPARE
    )
    tables[16:24] = jnp.minimum(in_places, COLS - 1) * ROW
    tables[24:32] = jnp.where(slot < coming, base + slot * FIELDS, SPARE)
    info[...] = jnp.where(slot == 0, leaving, coming)
    leaving, coming = (pltpu.roll(one, PEERS - me, 1) for one in (info[0:1], info[1:2]))
    total = leaving + coming
    blocked = wrap(peer) * 2 % PEERS == 0
    excess = jnp.maximum(total - SLOTS, 0)
    room = jnp.minimum(jnp.maximum(SLOTS - total, 0), RELAYS)
    tables[32:40] = jnp.where(
        slot == FACTS,
        leaving | (coming << 4) | (excess << 8),
        jnp.where(slot == ROOM, jnp.where(blocked, 0, room), blocked.astype(jnp.int32)),
    )


def make_plan(table, plan):
    facts, room, used = (table.at[32 + i] for i in (FACTS, ROOM, USED))

    def offset(o, carry):
        fact = facts[o]
        leaving = fact & 15
        coming = (fact >> 4) & 15
        excess = fact >> 8
        middle = o == PEERS // 2

        def column(t, carry):
            last, count, failed = carry

            def search(state):
                tries, u, _ = state
                u = wrap(u + 1)
                return tries + 1, u, (room[u] == 0) | (used[wrap(o - u)] > 0)

            _, u, taken = lax.while_loop(
                lambda state: state[2] & (state[0] < PEERS), search,
                (jnp.int32(0), last, jnp.bool_(True)),
            )
            found = jnp.logical_not(taken)
            slot = leaving - excess + jnp.where(middle, 2 * t, t)
            mirror_slot = jnp.where(middle, slot + 1, coming - excess + t)
            both = jnp.logical_not(middle) | (2 * t + 1 < excess)

            @pl.when(found)
            def _():
                free = room[u]
                r = SLOTS - free
                room[u] = free - 1
                room[PEERS - u] = free - 1
                used[wrap(o - u)] = 1
                used[wrap(u - o)] = 1
                plan[count] = o | (u << 7) | (r << 14) | (slot << 18)
                plan[count + 1] = (PEERS - o) | ((PEERS - u) << 7) | (r << 14) | (mirror_slot << 18)

            count = count + jnp.where(found, jnp.where(both, 2, 1), 0)
            return u, count, failed | taken.astype(jnp.int32)

        rounds = jnp.where(middle, (excess + 1) >> 1, excess)
        return lax.fori_loop(0, rounds, column, carry)

    zero = jnp.int32(0)
    _, count, failed = lax.fori_loop(1, PEERS // 2 + 1, offset, (zero, zero, zero))
    plan[PLAN_COUNT] = count
    plan[PLAN_FAILED] = failed


def planned(plan, i):
    entry = plan[i]
    o = entry & 127
    u = (entry >> 7) & 127
    return o, u, (entry >> 14) & 15, (entry >> 18) & 15


def pack_kernel(
    departing, arriving, x, inc, rates, sunlit, eddy, send, plan, info,
    x_tiles, inc_tiles, x_rows, inc_rows, packed, tables, places, sems, table_sem,
):
    parts = 4
    x_copies = copy_chunks(chunked(x, x_tiles, parts), sems, 0)
    inc_copies = copy_chunks(chunked(inc, inc_tiles, parts), sems, parts)
    me = device_index()
    fill_tables(me, departing, arriving, tables, info)
    move = pltpu.make_async_copy(tables, places, table_sem.at[0])
    move.start()
    spread_scalars(rates, sunlit, eddy, inc_rows)
    move.wait()
    make_plan(places, plan)
    count = COLS // 8 // parts
    for copies, tiles, rows in ((x_copies, x_tiles, x_rows), (inc_copies, inc_tiles, inc_rows)):
        for i, one in enumerate(copies):
            one.wait()
            spread_rows(tiles, rows, i * count, count)

    def relay(i, carry):
        o, u, r, c = planned(plan, i)
        source = places[c, wrap(me + o)]
        target = wrap(me + u) * MESSAGE + r * FIELDS
        packed[pl.ds(target, FIELDS), :] = x_rows[pl.ds(source, FIELDS), :]
        return carry

    lax.fori_loop(0, plan[PLAN_COUNT], relay, 0)
    group = lax.broadcasted_iota(jnp.int32, (1, LEV), 1) >> 3

    def body(p, carry):
        scalars = jnp.zeros((1, LEV), jnp.float32)
        for c in range(CAP):
            packed[pl.ds(places[8 + c, p], FIELDS), :] = x_rows[pl.ds(places[c, p], FIELDS), :]
            row = places[16 + c, p]
            packed[pl.ds(places[24 + c, p], FIELDS), :] = inc_rows[pl.ds(row, FIELDS), :]
            scalars = jnp.where(group == c, inc_rows[pl.ds(row + FIELDS, 1), :], scalars)
        packed[pl.ds(p * MESSAGE + SCALARS_AT, 1), :] = scalars
        return carry

    parts = 4
    step = PEERS // parts
    size = step * MESSAGE
    copies = []
    for i in range(parts):
        lax.fori_loop(i * step, (i + 1) * step, body, 0)
        part = pl.ds(i * size, size)
        copies += copy_chunks([(packed.at[part], send.at[part])], sems, i)
    for one in copies:
        one.wait()


def relay_kernel(plan, recv, prepared, send, landed, sems):
    del prepared
    me = device_index()
    first = (SLOTS - RELAYS) * FIELDS // 8 * 8
    (copy,) = copy_chunks([(recv.at[:, pl.ds(first, MESSAGE - first), :], landed)], sems, 0)
    copy.wait()

    def forward(i, carry):
        o, u, r, _ = planned(plan, i)
        row = landed[wrap(me - u), pl.ds(r * FIELDS - first, FIELDS), :]
        send[pl.ds(wrap(me + o - u) * HOP, FIELDS), :] = row
        return carry

    lax.fori_loop(0, plan[PLAN_COUNT], forward, 0)


def resend_kernel(departing, x, send, x_tiles, x_rows, packed, sems):
    (copy,) = copy_chunks([(x, x_tiles)], sems, 0)
    copy.wait()
    spread_rows(x_tiles, x_rows, 0, COLS // 8)

    def body(p, carry):
        for c in range(CAP):
            j = jnp.minimum(departing[c, p], COLS - 1)
            packed[pl.ds(p * RESENT + c * FIELDS, FIELDS), :] = x_rows[pl.ds(j * ROW, FIELDS), :]
        return carry

    lax.fori_loop(0, PEERS, body, 0)
    (copy,) = copy_chunks([(packed, send)], sems, 0)
    copy.wait()


def resident_kernel(
    staying, x, inc, rates, sunlit, eddy, span_x, block_inc, x_turned, inc_turned, stable,
    x_tiles, inc_tiles, x_rows, inc_rows, sems,
):
    load_rows(x, inc, rates, sunlit, eddy, x_tiles, inc_tiles, x_rows, inc_rows, sems)

    def body(t, carry):
        for i in range(8):
            j = t * 8 + i
            q = staying[j]
            span_x[pl.ds(q * ROW, FIELDS), :] = x_rows[pl.ds(j * ROW, FIELDS), :]
            source = jnp.minimum(q, COLS - 1)
            block_inc[pl.ds(j * ROW, ROW), :] = inc_rows[pl.ds(source * ROW, ROW), :]
        return carry

    lax.fori_loop(0, COLS // 8, body, 0)
    turn(lambda g, f: tile_block(x_tiles, g, f), x_turned)
    turn(lambda g, f: tile_block(inc_tiles, g, f), inc_turned)

    def state(k):
        return [level(x_turned, f, k) for f in RICHARDSON]

    def interface(k, above):
        below = state(k + 1)
        stable[k] = stability_between(above, below)
        return below

    lax.fori_loop(0, LEV - 1, interface, state(0), unroll=2)
    stable[LEV - 1] = jnp.zeros((8, LEV), jnp.float32)


def tile_block(tiles, g, f):
    return jnp.concatenate(
        [tiles[pl.ds((g * 16 + i) * 48 + f * 8, 8), :] for i in range(16)], axis=0
    )


def row_block(rows, g, f):
    return jnp.concatenate(
        [rows[pl.ds((g * 128 + i * 8) * ROW + f, 8, stride=ROW), :] for i in range(16)], axis=0
    )


def turn(load, turned):
    def body(g, carry):
        for f in range(FIELDS):
            turned[f, pl.ds(g * GROUP, LEV), :] = load(g, f).T
        return carry

    lax.fori_loop(0, 8, body, 0)


def turn_onto(load, right, wind=None):
    def body(g, carry):
        for f in range(FIELDS):
            lines = pl.ds(g * GROUP, LEV)
            block = load(g, f).T
            if wind is not None and f in RICHARDSON:
                wind[RICHARDSON[f], lines, :] = block
            right[f, lines, :] = right[f, lines, :] + block
        return carry

    lax.fori_loop(0, 8, body, 0)


def transpose_out(right, tiles, out, sems):
    copies = []
    for g, pair in enumerate(chunked(tiles, out, 8)):
        def body(f, carry):
            block = right[f, pl.ds(g * GROUP, LEV), :].T
            for i in range(16):
                tiles[pl.ds((g * 16 + i) * 48 + f * 8, 8), :] = block[i * 8 : (i + 1) * 8]
            return carry

        lax.fori_loop(0, FIELDS, body, 0, unroll=True)
        copies += copy_chunks([pair], sems, g)
    return copies


def level(ref, f, k):
    return ref[f, pl.ds(k, 8, stride=GROUP), :]


def put_level(ref, f, k, value):
    ref[f, pl.ds(k, 8, stride=GROUP), :] = value


def stability_between(upper, lower):
    lapse = upper[0] - lower[0]
    u = upper[1] - lower[1]
    v = upper[2] - lower[2]
    shear = u * u + v * v + 0.1
    unstable = lapse < 0.0
    stable_root = shear + 10.0 * lapse
    top = jnp.where(unstable, shear - 8.0 * lapse, shear * shear)
    bottom = jnp.where(unstable, shear - lapse, stable_root * stable_root)
    return top / bottom


def weight_pair(eddy, stability):
    wind = eddy * stability
    return (1.35 * wind, wind)


def wind_state(wind):
    return lambda k: [level(wind, i, k) for i in range(3)]


def solve(right, factor, forcing, eddy, state, stability):
    for f in range(FIELDS):
        put_level(right, f, LEV - 1, level(right, f, LEV - 1) + forcing[f])

    zero = jnp.zeros((8, 128), jnp.float32)

    def eliminate(i, carry):
        excess, moved, above, below = carry
        ks = (i, LEV - 1 - i)
        inner = (state(i + 1), state(LEV - 2 - i))
        weights = (
            weight_pair(eddy, stability(above, inner[0], i)),
            weight_pair(eddy, stability(inner[1], below, LEV - 2 - i)),
        )
        new_excess = [[], []]
        new_moved = [[], []]
        for side in range(2):
            ratio = []
            inverse = []
            for m in range(2):
                base = 1.0 + excess[side][m]
                inv = 1.0 / (base + weights[side][m])
                out = weights[side][m] * inv
                factor[side, m, i] = out
                ratio.append(out)
                inverse.append(inv)
                new_excess[side].append(base * out)
            for f in range(FIELDS):
                m = 0 if f in HEAT else 1
                z = level(right, f, ks[side]) + moved[side][f]
                put_level(right, f, ks[side], z * inverse[m])
                new_moved[side].append(z * ratio[m])
        return new_excess, new_moved, inner[0], inner[1]

    start = ([[zero] * 2] * 2, [[zero] * FIELDS] * 2, state(0), state(LEV - 1))
    half = LEV // 2
    excess, moved, above, below = lax.fori_loop(0, half - 1, eliminate, start, unroll=3)
    weight = weight_pair(eddy, stability(above, below, half - 1))
    solved = [[], []]
    for f in range(FIELDS):
        m = 0 if f in HEAT else 1
        w = weight[m]
        a = 1.0 + excess[0][m]
        b = 1.0 + excess[1][m]
        inv = 1.0 / (a * b + w * (a + b))
        za = level(right, f, half - 1) + moved[0][f]
        zb = level(right, f, half) + moved[1][f]
        ya = ((b + w) * za + w * zb) * inv
        yb = ((a + w) * zb + w * za) * inv
        put_level(right, f, half - 1, ya)
        put_level(right, f, half, yb)
        solved[0].append(ya)
        solved[1].append(yb)

    def substitute(i, carry):
        step = half - 2 - i
        ks = (step, LEV - 1 - step)
        new = [[], []]
        for side in range(2):
            ratio = [factor[side, m, step] for m in range(2)]
            for f in range(FIELDS):
                m = 0 if f in HEAT else 1
                y = level(right, f, ks[side]) + ratio[m] * carry[side][f]
                put_level(right, f, ks[side], y)
                new[side].append(y)
        return new

    lax.fori_loop(0, half - 1, substitute, solved, unroll=3)


def land(copies, put):
    step = PEERS // len(copies)
    for i, group in enumerate(copies):
        for one in group:
            one.wait()
        lax.fori_loop(i * step, (i + 1) * step, put, 0)


def block_kernel(
    departing, edges, x_turned, stable_in, rows_in, recv, out, left_rows, right_rows,
    tiles, rows, landed, landed_scalars, turned, stable, right, factor, scalars, sems,
):
    parts = 4
    step = PEERS // parts
    (first,) = copy_chunks([(rows_in, rows)], sems, 0)

    def part(i, offset, size, target):
        peers = pl.ds(i * step, step)
        return recv.at[peers, pl.ds(offset, size), :], target.at[peers]

    head = (SCALARS_AT // 8) * 8
    (turn,) = copy_chunks([(recv.at[:, pl.ds(head, 8), :], landed_scalars)], sems, 1)
    arrivals = copy_chunks([part(i, 0, CAP * FIELDS, landed) for i in range(parts)], sems, 2)
    last = copy_chunks([(x_turned, right), (stable_in, stable)], sems, 2 + parts)
    turn.wait()
    for i in range(PEERS // 8):
        lines = landed_scalars[pl.ds(i * 8, 8), SCALARS_AT - head, :]
        for c in range(CAP):
            turned[c, pl.ds(i * 8, 8), :] = pltpu.roll(lines, (LEV - 8 * c) % LEV, 1)
    first.wait()

    def put(p, carry):
        for c in range(CAP):
            row = departing[c, p] * ROW
            rows[pl.ds(row, FIELDS), :] = landed[p, pl.ds(c * FIELDS, FIELDS), :]
            rows[pl.ds(row + FIELDS, 1), :] = turned[c, pl.ds(p, 1), :]
        return carry

    land([[one] for one in arrivals], put)
    for one in last:
        one.wait()
    turn_onto(lambda g, f: row_block(rows, g, f), right)
    for g in range(8):
        scalars[0, pl.ds(g * GROUP, LEV), :] = row_block(rows, g, FIELDS).T
    solve(
        right, factor,
        [level(scalars, 0, f) for f in range(FIELDS)],
        level(scalars, 0, FIELDS),
        lambda k: [],
        lambda upper, lower, k: stable[k],
    )
    copies = transpose_out(right, tiles, out, sems)

    def edge(k, carry):
        for side, edge_out in ((0, left_rows), (1, right_rows)):
            j = edges[side, k]
            base = (j >> 3) * 48 + (j & 7)
            edge_out[pl.ds(k * FIELDS, FIELDS), :] = tiles[pl.ds(base, FIELDS, stride=8), :]
        return carry

    lax.fori_loop(0, EDGE, edge, 0, unroll=4)
    for one in copies:
        one.wait()


def span_half(tiles, rows, rates, sunlit, eddy, out, wind, right, factor, sems):
    turn_onto(lambda g, f: row_block(rows, g, f), right, wind)
    lit = 0.5 + sunlit[...].astype(jnp.float32)
    forcing = [
        jnp.concatenate([rates[pl.ds(f, 1), pl.ds(g * 128, 128)] for g in range(8)], axis=0) * lit
        for f in range(FIELDS)
    ]
    solve(
        right, factor, forcing, eddy[...], wind_state(wind),
        lambda upper, lower, k: stability_between(upper, lower),
    )
    for one in transpose_out(right, tiles, out, sems):
        one.wait()


def span_kernel(
    arriving, plan, info, inc_turned, rates, sunlit, eddy, rows_in, recv, hop, out,
    tiles, rows, landed, landed_hop, wind, right, factor, sems,
):
    parts = 4
    size = PEERS // parts * MESSAGE
    (first,) = copy_chunks([(rows_in, rows)], sems, 0)
    blocks = [pl.ds(i * size, size) for i in range(parts)]
    arrivals = copy_chunks([(recv.at[one], landed.at[one]) for one in blocks], sems, 1)
    relayed, last = copy_chunks([(hop, landed_hop), (inc_turned, right)], sems, 1 + parts)
    first.wait()

    def put(p, carry):
        ahead = info[0, p]
        base = p * MESSAGE + ahead * FIELDS
        for c in range(CAP):
            q = jnp.where(ahead + c < SLOTS, arriving[c, p], DUMP)
            rows[pl.ds(q * ROW, FIELDS), :] = landed[pl.ds(base + c * FIELDS, FIELDS), :]
        return carry

    land([[one] for one in arrivals], put)
    relayed.wait()
    me = device_index()

    def put_relayed(i, carry):
        o, u, _, c = planned(plan, i)
        q = arriving[c, wrap(me - o)]
        source = wrap(me - o + u) * HOP
        rows[pl.ds(q * ROW, FIELDS), :] = landed_hop[pl.ds(source, FIELDS), :]
        return carry

    lax.fori_loop(0, plan[PLAN_COUNT], put_relayed, 0)
    last.wait()
    span_half(tiles, rows, rates, sunlit, eddy, out, wind, right, factor, sems)


def resent_span_kernel(
    arriving, inc_turned, rates, sunlit, eddy, rows_in, recv, out,
    tiles, rows, landed, wind, right, factor, sems,
):
    for one in copy_chunks([(rows_in, rows), (recv, landed), (inc_turned, right)], sems, 0):
        one.wait()

    def put(p, carry):
        for c in range(CAP):
            q = arriving[c, p]
            rows[pl.ds(q * ROW, FIELDS), :] = landed[pl.ds(p * RESENT + c * FIELDS, FIELDS), :]
        return carry

    lax.fori_loop(0, PEERS, put, 0)
    span_half(tiles, rows, rates, sunlit, eddy, out, wind, right, factor, sems)


def average_kernel(
    edges, column, own_left, own_right, far_left, far_right, after, out, buf, sides, sems
):
    del after
    load = copy_chunks(
        [(one, sides.at[i]) for i, one in enumerate((own_left, far_left, own_right, far_right))],
        sems, 1,
    )
    load += copy_chunks([(column, buf)], sems, 0)
    for one in load[:4]:
        one.wait()
    for side in range(2):
        sides[2 * side] = (sides[2 * side] + sides[2 * side + 1]) * 0.5
    load[4].wait()

    def body(k, carry):
        for side in range(2):
            j = edges[side, k]
            base = (j >> 3) * 48 + (j & 7)
            buf[pl.ds(base, FIELDS, stride=8), :] = sides[2 * side, pl.ds(k * FIELDS, FIELDS), :]
        return carry

    lax.fori_loop(0, EDGE, body, 0, unroll=8)
    for one in copy_chunks(chunked(buf, out, 4), sems, 0):
        one.wait()


def shape(*dims, dtype=jnp.float32):
    return jax.ShapeDtypeStruct(dims, dtype)


def spec(space):
    return pl.BlockSpec(memory_space=space)


def cost(flops, mib):
    return pl.CostEstimate(flops=flops, bytes_accessed=mib * 2**20, transcendentals=0)


def call(kernel, operands, outputs, scratch, sem_count, estimate, more=()):
    return pl.pallas_call(
        kernel,
        out_shape=tuple(one for _, one in outputs),
        in_specs=[spec(space) for space, _ in operands],
        out_specs=tuple(spec(space) for space, _ in outputs),
        scratch_shapes=[
            *(pltpu.VMEM(dims, jnp.float32) for dims in scratch),
            *more,
            pltpu.SemaphoreType.DMA((sem_count,)),
        ],
        compiler_params=pltpu.CompilerParams(vmem_limit_bytes=VMEM_LIMIT),
        cost_estimate=estimate,
    )(*(array for _, array in operands))


def exchange(rows, sublanes):
    return lax.all_to_all(
        rows.reshape(PEERS, sublanes, LEV), ("blk", "sub"), split_axis=0, concat_axis=0, tiled=True
    )


def on_device(
    dynamics_profile_values,
    parameterized_increments,
    ground_exchange_rates,
    sunlit_indicator,
    eddy_coefficient_scale,
    departing_profile_indices,
    arriving_parcel_places,
    resident_parcel_place,
    boundary_profile_indices,
):
    smem, vmem, hbm = pltpu.SMEM, pltpu.VMEM, pl.ANY
    departing = (smem, departing_profile_indices[0].T)
    arriving = (smem, arriving_parcel_places[0].T)
    staying = (smem, resident_parcel_place.reshape(-1))
    edges = (smem, boundary_profile_indices[0])
    x = (hbm, to_tiles(dynamics_profile_values))
    inc = (hbm, to_tiles(parameterized_increments))
    physics = (
        (vmem, ground_exchange_rates),
        (vmem, sunlit_indicator.reshape(8, LEV)),
        (vmem, eddy_coefficient_scale.reshape(8, LEV)),
    )
    whole = (COLS * FIELDS, LEV)
    rows = (ROWS_ALLOC, LEV)
    side = (EDGE * FIELDS, LEV)
    stable_dims = (LEV, 8, LEV)
    transposed = ((3, 8 * GROUP, LEV), (FIELDS, 8 * GROUP, LEV), (2, 2, LEV // 2, 8, LEV))

    integers = pltpu.VMEM((40, PEERS), jnp.int32)

    send, plan, info = call(
        pack_kernel, ((vmem, departing[1]), (vmem, arriving[1]), x, inc, *physics),
        (
            (hbm, shape(SPARE, LEV)),
            (smem, shape(PLAN, dtype=jnp.int32)),
            (vmem, shape(CAP, PEERS, dtype=jnp.int32)),
        ),
        (whole, whole, rows, rows, (PACKED, LEV)), 1, cost(0, 14),
        (
            integers,
            pltpu.SMEM((40, PEERS), jnp.int32),
            pltpu.SemaphoreType.DMA((8,)),
        ),
    )
    plan = (smem, plan)
    recv = exchange(send, MESSAGE)
    span_rows, block_rows, x_turned, inc_turned, stable = call(
        resident_kernel, (staying, x, inc, *physics),
        tuple((vmem, shape(*dims)) for dims in (rows, rows, transposed[1], transposed[1], stable_dims)),
        (whole, whole, rows, rows), 8, cost(0, 14),
    )
    failed, block_rows = lax.optimization_barrier((plan[1][PLAN_FAILED], block_rows))
    (hop,) = call(
        relay_kernel, (plan, (hbm, recv), (hbm, block_rows)), ((vmem, shape(PEERS * HOP, LEV)),),
        ((PEERS, MESSAGE - (SLOTS - RELAYS) * FIELDS // 8 * 8, LEV),), 1, cost(0, 2),
    )
    hop = exchange(hop, HOP)
    column, left_rows, right_rows = call(
        block_kernel,
        (departing, edges, *((hbm, one) for one in (x_turned, stable, block_rows, recv))),
        ((hbm, shape(*whole)), (vmem, shape(*side)), (vmem, shape(*side))),
        (
            whole, rows, (PEERS, CAP * FIELDS, LEV), (PEERS, 8, LEV), (CAP, PEERS, LEV),
            stable_dims, *transposed[1:], (1, 8 * GROUP, LEV),
        ),
        12, cost(10**9, 20),
    )
    count = lax.axis_size("blk")
    far_left = lax.ppermute(right_rows, "blk", [(i, (i + 1) % count) for i in range(count)])
    far_right = lax.ppermute(left_rows, "blk", [((i + 1) % count, i) for i in range(count)])

    def relayed():
        return call(
            span_kernel,
            (
                arriving, plan, (smem, info), (hbm, inc_turned), *physics, (hbm, span_rows),
                (hbm, recv.reshape(SPARE, LEV)), (hbm, hop.reshape(PEERS * HOP, LEV)),
            ),
            ((hbm, shape(*whole)),),
            (whole, rows, (LANDED, LEV), (PEERS * HOP, LEV), *transposed), 11, cost(10**9, 20),
        )[0]

    def resent():
        sent = (PEERS * RESENT, LEV)
        (again,) = call(
            resend_kernel, (departing, x), ((hbm, shape(*sent)),), (whole, rows, sent), 1, cost(0, 8)
        )
        again = exchange(again, RESENT).reshape(sent)
        return call(
            resent_span_kernel,
            (arriving, (hbm, inc_turned), *physics, (hbm, span_rows), (hbm, again)),
            ((hbm, shape(*whole)),), (whole, rows, sent, *transposed), 8, cost(10**9, 20),
        )[0]

    span_out = lax.cond(failed > 0, resent, relayed)
    (column,) = call(
        average_kernel,
        (edges, *((hbm, one) for one in (column, left_rows, right_rows, far_left, far_right, span_out))),
        ((hbm, shape(*whole)),),
        (whole, (4, *side)), 5, cost(0, 8),
    )
    return from_tiles(span_out), from_tiles(column)


def solution(mesh):
    one = P(("blk", "sub"))
    placed = (one, one, P(None, ("blk", "sub")), one, one, one, one, one, one)
    return jax.shard_map(
        on_device, mesh=mesh, in_specs=placed, out_specs=(one, one), check_vma=False
    )
```
